32 devices in a mesh: group: 8 (over y, x, core), tp: 4 (over z).
Axes of the slice: x: 2, y: 2, z: 4, core: 2. Of those that a mesh axis runs over, the one named last changes fastest.
Arguments:
- queries: bfloat16 [128, 8192], P('group', 'tp'), may hold values from -100 to 100
- cache_keys: bfloat16 [128, 512, 1024], P('group', None, 'tp'), may hold values from -6 to 6
- cache_values: bfloat16 [128, 512, 1024], P('group', None, 'tp'), may hold values from -6 to 6
- pool_keys: bfloat16 [16, 4096, 1024], P('group', None, 'tp'), may hold values from -6 to 6
- pool_values: bfloat16 [16, 4096, 1024], P('group', None, 'tp'), may hold values from -6 to 6
- row_lengths: int32 [128], P('group'), may hold values from 2 to 49664, as said below
- slot_owner: int32 [16], P('group'), may hold values from -1 to 127, as said below
- slot_fill: int32 [16], P('group'), may hold values from 0 to 4096, as said below
- free_counts: int32 [8], P('group'), may hold values from 0 to 2047
- out_weight: bfloat16 [8192, 8192], P('tp'), may hold values from -0.0625 to 0.0625
Outputs:
- mixed_out: bfloat16 [128, 8192], P('group', 'tp')
- total_free: int32 [1], replicated
The draws below stay inside these ranges and needn't reach their ends.
Inputs may be any that keep to these rules, and one draw needn't show every extreme that they name: `row_lengths`: A row of length over 512 has the rest of its positions in the slots it owns, so its length is 512 plus the sum of their slot_fill; other rows own no slot. `slot_owner`: each slot is free or holds one block of one row; slots may sit in any group, the row's own too. `slot_fill`: A free slot has fill 0, an owned one at least 2.
All inputs are finite; a program needn't handle non-finite values.
Results may differ from the reference program's by a relative error of at most 0.0066.
Values may be sent and summed in bfloat16 or wider, within the bound.
No kernel may reach another device: no remote copies, remote signals or barrier semaphores. Data moves between devices by JAX's collectives and lax.ppermute only.
A program may use at most 128 MiB of HBM per device.

```python
import math
import jax
import jax.numpy as jnp
from jax import lax

D = 8192
HEADS = 64
KV_HEADS = 8
HEAD_DIM = 128
CAP = 512
BLOCK = 4096
LONG_BLOCKS = 12
GROUPS = 8
LONG_ROWS = 1
TOTAL_ROWS = 128
SLOTS_ALL = 16


def drawn_keys(key, drawn):
    return drawn


def draw_queries(key, part):
    drawn = jnp.clip(2.0 * jax.random.normal(jax.random.fold_in(key, 33), (TOTAL_ROWS, HEADS, HEAD_DIM), jnp.float32), -12.0, 12.0)
    return drawn.reshape(TOTAL_ROWS, HEADS * HEAD_DIM).astype(jnp.bfloat16)


def draw_cache_keys(key, part):
    drawn = jnp.clip(jax.random.normal(jax.random.fold_in(key, 31), (TOTAL_ROWS, CAP, KV_HEADS * HEAD_DIM), jnp.float32), -6.0, 6.0)
    return drawn_keys(key, drawn).astype(jnp.bfloat16)


def draw_pool_keys(key, part):
    drawn = jnp.clip(jax.random.normal(jax.random.fold_in(key, 32), (SLOTS_ALL, BLOCK, KV_HEADS * HEAD_DIM), jnp.float32), -6.0, 6.0)
    return drawn_keys(key, drawn).astype(jnp.bfloat16)


def layout(key):
    others = jax.random.permutation(jax.random.fold_in(key, 11), TOTAL_ROWS - 1)[:LONG_ROWS - 1].astype(jnp.int32)
    long_rows = jnp.concatenate([jnp.full((1,), TOTAL_ROWS - 1, jnp.int32), others])
    placed = jax.random.permutation(jax.random.fold_in(key, 12), SLOTS_ALL)[:LONG_ROWS * LONG_BLOCKS].astype(jnp.int32)
    last_fill = jax.random.randint(jax.random.fold_in(key, 13), (LONG_ROWS,), 2, BLOCK + 1).astype(jnp.int32)
    short_len = jax.random.randint(jax.random.fold_in(key, 14), (TOTAL_ROWS,), 2, CAP + 1).astype(jnp.int32)
    lengths = short_len.at[long_rows].set(CAP + (LONG_BLOCKS - 1) * BLOCK + last_fill)
    owners = jnp.full((SLOTS_ALL,), -1, jnp.int32).at[placed].set(jnp.repeat(long_rows, LONG_BLOCKS))
    block_fill = jnp.full((LONG_ROWS, LONG_BLOCKS), BLOCK, jnp.int32).at[:, LONG_BLOCKS - 1].set(last_fill).reshape(-1)
    filled = jnp.zeros((SLOTS_ALL,), jnp.int32).at[placed].set(block_fill)
    return (lengths, owners, filled)


def draw_row_lengths(key, part):
    return layout(key)[0]


def draw_slot_owner(key, part):
    return layout(key)[1]


def draw_slot_fill(key, part):
    return layout(key)[2]


def draw_free_counts(key, part):
    levels = jax.random.randint(jax.random.fold_in(key, 22), (GROUPS,), 1, 12).astype(jnp.int32)
    reach = jnp.left_shift(jnp.ones((GROUPS,), jnp.int32), levels)
    spread = jax.random.randint(jax.random.fold_in(key, 21), (GROUPS,), 0, 2048).astype(jnp.int32)
    spread = jnp.remainder(spread, reach).astype(jnp.int32)
    return spread.at[GROUPS - 1].set(2047).at[0].set(0).astype(jnp.int32)


def block_levels(rng, dims, shards, least, top_value):
    factor_of = 1.0
    for axis_at, shards_of in shards:
        steps = jax.random.uniform(jax.random.fold_in(jax.random.fold_in(rng, 6), axis_at), (shards_of,), jnp.float32, least / len(shards), top_value / len(shards))
        factor_of = factor_of * jnp.repeat(jnp.exp(steps), dims[axis_at] // shards_of).reshape((-1,) + (1,) * (len(dims) - 1 - axis_at))
    return factor_of


def noise(own_key, extent, scale, bound, cuts=(), kind=jnp.bfloat16):
    array = jax.random.normal(own_key, extent, jnp.float32) * scale
    if len(cuts) > 0:
        array = block_levels(own_key, extent, cuts, -0.22, 0.18) * array
    return jnp.clip(array, min=-bound, max=bound).astype(kind)


def setup_inputs(seed: int = 0) -> dict:
    splits = jax.random.split(jax.random.key(seed), 11)
    queries = draw_queries(jax.random.fold_in(splits[10], 71), 0)
    cache_keys = draw_cache_keys(jax.random.fold_in(splits[10], 71), 0)
    cache_values = noise(splits[2], (TOTAL_ROWS, CAP, KV_HEADS * HEAD_DIM), 1.0, 6.0, ((0, 8), (2, 4)))
    pool_keys = draw_pool_keys(jax.random.fold_in(splits[10], 71), 0)
    pool_values = noise(splits[4], (SLOTS_ALL, BLOCK, KV_HEADS * HEAD_DIM), 1.0, 6.0, ((0, 8), (2, 4)))
    row_lengths = draw_row_lengths(jax.random.fold_in(splits[10], 71), 0)
    slot_owner = draw_slot_owner(jax.random.fold_in(splits[10], 71), 0)
    slot_fill = draw_slot_fill(jax.random.fold_in(splits[10], 71), 0)
    free_counts = draw_free_counts(jax.random.fold_in(splits[10], 71), 0)
    out_weight = noise(splits[9], (HEADS * HEAD_DIM, D), (HEADS * HEAD_DIM) ** -0.5, 0.0625, ((0, 4),))
    return dict(queries=queries, cache_keys=cache_keys, cache_values=cache_values, pool_keys=pool_keys, pool_values=pool_values, row_lengths=row_lengths, slot_owner=slot_owner, slot_fill=slot_fill, free_counts=free_counts, out_weight=out_weight)


far_below = -1e+30

def partial_attention(queries, key_block, values, live_count):
    batch_rows, positions = (key_block.shape[0], key_block.shape[1])
    kv_heads = key_block.shape[2] // HEAD_DIM
    query_heads = queries.shape[1] // HEAD_DIM
    query_split = queries.reshape(batch_rows, kv_heads, query_heads // kv_heads, HEAD_DIM).astype(jnp.float32)
    key_split = key_block.reshape(batch_rows, positions, kv_heads, HEAD_DIM).astype(jnp.float32)
    value_split = values.reshape(batch_rows, positions, kv_heads, HEAD_DIM).astype(jnp.float32)
    scores = jnp.einsum('nkgd,nlkd->nkgl', query_split, key_split) / math.sqrt(HEAD_DIM)
    visible = (jnp.arange(positions, dtype=jnp.int32)[None, :] < live_count[:, None])[:, None, None, :]
    scores = jnp.where(visible, scores, far_below)
    highest = lax.optimization_barrier(jnp.max(scores, axis=-1))
    weights = jnp.where(visible, jnp.exp(scores - highest[..., None]), 0.0)
    weight_sum = lax.optimization_barrier(jnp.sum(weights, axis=-1))
    rounded = weights.astype(jnp.bfloat16).astype(jnp.float32)
    mixed = jnp.einsum('nkgl,nlkd->nkgd', rounded, value_split)
    return (highest.reshape(batch_rows, query_heads), weight_sum.reshape(batch_rows, query_heads), mixed.reshape(batch_rows, query_heads, HEAD_DIM))

def one_row(single):
    query_row, key_rows, value_rows, live_count = single
    highest, weight_sum, mixed = partial_attention(query_row[None], key_rows[None], value_rows[None], live_count[None])
    return (highest[0], weight_sum[0], mixed[0])

def reference(queries, cache_keys, cache_values, pool_keys, pool_values, row_lengths, slot_owner, slot_fill, free_counts, out_weight):
    local_high, local_total, local_mixed = lax.map(one_row, (queries, cache_keys, cache_values, jnp.minimum(row_lengths, CAP).astype(jnp.int32)))
    chosen = queries[jnp.maximum(slot_owner, 0).astype(jnp.int32)]
    slot_high, slot_total, slot_mixed = lax.map(one_row, (chosen, pool_keys, pool_values, slot_fill))
    row_count = queries.shape[0]
    matched = (jnp.arange(row_count, dtype=jnp.int32)[:, None] == slot_owner[None, :])[:, :, None]
    far_high = lax.optimization_barrier(jnp.max(jnp.where(matched, slot_high[None], far_below), axis=1))
    factor = jnp.where(matched, jnp.exp(slot_high[None] - far_high[:, None]), 0.0)
    far_total = lax.optimization_barrier(jnp.sum(factor * slot_total[None], axis=1))
    far_mixed = jnp.einsum('rsh,shd->rhd', factor, slot_mixed, precision=lax.Precision.HIGHEST)
    peak = jnp.maximum(local_high, far_high)
    near_scale = jnp.exp(local_high - peak)
    far_scale = jnp.exp(far_high - peak)
    attended = (near_scale[..., None] * local_mixed + far_scale[..., None] * far_mixed) / (near_scale * local_total + far_scale * far_total)[..., None]
    attended = attended.reshape(row_count, -1).astype(jnp.bfloat16)
    mixed_out = jnp.dot(attended, out_weight, preferred_element_type=jnp.float32).astype(jnp.bfloat16)
    total_free = jnp.sum(free_counts).astype(jnp.int32).reshape(1)
    return (mixed_out, total_free)
```

```python
import math

import jax
import jax.numpy as jnp
from jax import lax
from jax.experimental import pallas as pl
from jax.experimental.pallas import tpu as pltpu
from jax.sharding import PartitionSpec as P

HEAD_DIM = 128
LANES = 128
far_below = -1e30


VMEM = pl.BlockSpec(memory_space=pltpu.VMEM)
SMEM = pl.BlockSpec(memory_space=pltpu.SMEM)
f32 = jnp.float32
bf16 = jnp.bfloat16


def call(kernel, outs, ins, scratch=(), out_specs=None, flops=0, moved=0, vmem=8 << 20):
    return pl.pallas_call(
        kernel,
        out_shape=outs,
        in_specs=ins,
        out_specs=out_specs if out_specs is not None else jax.tree.map(lambda _: VMEM, outs),
        scratch_shapes=scratch,
        cost_estimate=pl.CostEstimate(flops=flops, bytes_accessed=moved, transcendentals=0),
        compiler_params=pltpu.CompilerParams(vmem_limit_bytes=vmem),
    )


def spread_heads(tile, kv_heads):
    if kv_heads == 1:
        return tile
    heads = tile.shape[0]
    owner = lax.broadcasted_iota(jnp.int32, tile.shape, 0) // (heads // kv_heads)
    return jnp.concatenate(
        [jnp.where(owner == k, tile, jnp.zeros_like(tile)) for k in range(kv_heads)], axis=1
    )


def own_columns(wide, kv_heads):
    if kv_heads == 1:
        return wide
    heads = wide.shape[0]
    owner = lax.broadcasted_iota(jnp.int32, (heads, HEAD_DIM), 0) // (heads // kv_heads)
    picked = wide[:, :HEAD_DIM]
    for k in range(1, kv_heads):
        picked = jnp.where(owner == k, wide[:, k * HEAD_DIM : (k + 1) * HEAD_DIM], picked)
    return picked


def scores_of(query, keys):
    return lax.dot_general(
        query, keys, (((1,), (1,)), ((), ())), preferred_element_type=f32
    ) * (1.0 / math.sqrt(HEAD_DIM))


def local_kernel(
    lengths, q_ref, keys, values, mixed_ref, high_ref, total_ref, q_heads, *, rows, heads, kv_heads
):
    positions = keys.shape[1]
    wide = q_ref[...].astype(f32)
    for h in range(heads):
        q_heads[pl.ds(h, rows, stride=heads), :] = wide[:, h * HEAD_DIM : (h + 1) * HEAD_DIM]
    place = lax.broadcasted_iota(jnp.int32, (heads, positions), 1)
    for r in range(rows):
        at = pl.ds(r * heads, heads)
        query = spread_heads(q_heads[at, :].astype(bf16), kv_heads)
        visible = place < lengths[r]
        scores = jnp.where(visible, scores_of(query, keys[r]), far_below)
        high = jnp.max(scores, axis=-1, keepdims=True)
        weights = jnp.where(visible, jnp.exp(scores - high), 0.0)
        total = jnp.sum(weights, axis=-1, keepdims=True)
        mixed = jnp.dot(weights.astype(bf16), values[r], preferred_element_type=f32)
        mixed_ref[at, :] = own_columns(mixed, kv_heads)
        high_ref[at, :] = jnp.broadcast_to(high, (heads, LANES))
        total_ref[at, :] = jnp.broadcast_to(total, (heads, LANES))


def slot_kernel(*refs, groups, rows, heads, kv_heads, slots, chunk):
    owners, fills, free = refs[:3]
    shards = refs[3 : 3 + groups]
    keys, values, _, packed, q_heads, scores = refs[3 + groups :]
    positions = keys.shape[1]
    me = lax.axis_index("group")
    row_at = lax.broadcasted_iota(jnp.int32, (rows, heads * HEAD_DIM), 0)
    for s in range(slots):
        owner = jnp.maximum(owners[s], 0)
        home = lax.div(owner, rows)
        row = lax.rem(owner, rows)
        for k in range(groups):

            @pl.when(jnp.bitwise_xor(home, me) == k)
            def _(k=k, s=s, row=row):
                block = jnp.where(row_at == row, shards[k][...].astype(f32), 0.0)
                single = jnp.sum(block, axis=0, keepdims=True)
                for h in range(heads):
                    q_heads[s * heads + h : s * heads + h + 1, :] = single[
                        :, h * HEAD_DIM : (h + 1) * HEAD_DIM
                    ]

    place = lax.broadcasted_iota(jnp.int32, (heads, positions), 1)
    lane = lax.broadcasted_iota(jnp.int32, (heads, LANES), 1)
    stats = jnp.where(lane == 3 * slots, free[0].astype(f32), 0.0)
    for s in range(slots):
        at = pl.ds(s * heads, heads)
        query = spread_heads(q_heads[at, :].astype(bf16), kv_heads)
        for c in range(0, positions, chunk):
            scores[at, c : c + chunk] = scores_of(query, keys[s, c : c + chunk, :])
    for s in range(slots):
        at = pl.ds(s * heads, heads)
        visible = place < fills[s]
        masked = jnp.where(visible, scores[at, :], far_below)
        high = jnp.max(masked, axis=-1, keepdims=True)
        weights = jnp.where(visible, jnp.exp(masked - high), 0.0)
        total = jnp.sum(weights, axis=-1, keepdims=True)
        mixed = jnp.dot(weights.astype(bf16), values[s], preferred_element_type=f32)
        packed[at, :] = own_columns(mixed, kv_heads)
        stats = jnp.where(lane == s, high, stats)
        stats = jnp.where(lane == slots + s, total, stats)
        stats = jnp.where(lane == 2 * slots + s, owners[s].astype(f32), stats)
    packed[slots * heads :, :] = stats


def project(x, weight, out, tp_mask, columns, chunk):
    start = jnp.bitwise_xor(lax.axis_index("tp"), tp_mask) * columns
    for c in range(0, columns, chunk):
        at = pl.ds(pl.multiple_of(start + c, chunk), chunk)
        out[:, c : c + chunk] = jnp.dot(
            x, weight[:, at], preferred_element_type=f32
        ).astype(out.dtype)


def combine_kernel(*refs, groups, rows, heads, slots, tp_mask, columns, chunk):
    mixed_ref, high_ref, total_ref = refs[:3]
    parts = refs[3 : 3 + groups]
    weight, x_ref, out, free_total, mixed, high, total = refs[3 + groups :]
    first = lax.axis_index("group") * rows
    mixed[...] = mixed_ref[...]
    high[...] = high_ref[...]
    total[...] = total_ref[...]
    free = jnp.zeros((heads, LANES), f32)
    for k in range(groups):
        stats = parts[k][slots * heads :, :]
        free = free + stats
        for s in range(slots):
            row = stats[0, 2 * slots + s].astype(jnp.int32) - first

            @pl.when((row >= 0) & (row < rows))
            def _(k=k, s=s, row=row, stats=stats):
                at = pl.ds(pl.multiple_of(row * heads, heads), heads)
                slot_high = jnp.broadcast_to(stats[:, s : s + 1], (heads, LANES))
                slot_total = jnp.broadcast_to(stats[:, slots + s : slots + s + 1], (heads, LANES))
                old = high[at, :]
                peak = jnp.maximum(old, slot_high)
                keep = jnp.exp(old - peak)
                add = jnp.exp(slot_high - peak)
                mixed[at, :] = keep * mixed[at, :] + add * parts[k][s * heads : (s + 1) * heads, :]
                total[at, :] = keep * total[at, :] + add * slot_total
                high[at, :] = peak

    free_total[0] = free[0, 3 * slots].astype(jnp.int32)
    mixed[...] = mixed[...] / total[...]
    for h in range(heads):
        x_ref[:, h * HEAD_DIM : (h + 1) * HEAD_DIM] = mixed[
            pl.ds(h, rows, stride=heads), :
        ].astype(bf16)
    project(x_ref[...], weight, out, tp_mask, columns, chunk)


def project_kernel(x_ref, weight, out, *, tp_mask, columns, chunk):
    project(x_ref[...], weight, out, tp_mask, columns, chunk)


def sum_kernel(*refs):
    total = refs[0][...]
    for part in refs[1:-1]:
        total = total + part[...].astype(f32)
    refs[-1][...] = total.astype(bf16)


def swap(value, axis, mask):
    size = lax.axis_size(axis)
    return lax.ppermute(value, axis, [(i, i ^ mask) for i in range(size)])


def gather_group(value):
    groups = lax.axis_size("group")
    found = [None] * groups
    found[0] = value
    found[1] = swap(value, "group", 1)
    for k in range(2, groups, 2):
        found[k] = swap(value, "group", k)
        found[k + 1] = swap(found[k], "group", 1)
    return found


def per_device(
    queries,
    cache_keys,
    cache_values,
    pool_keys,
    pool_values,
    row_lengths,
    slot_owner,
    slot_fill,
    free_counts,
    out_weight,
):
    groups, tp = lax.axis_size("group"), lax.axis_size("tp")
    rows, width = queries.shape
    heads = width // HEAD_DIM
    kv_heads = cache_keys.shape[2] // HEAD_DIM
    slots, positions = pool_keys.shape[:2]
    columns = out_weight.shape[1] // tp
    chunk = math.gcd(columns, 512)
    sizes = dict(rows=rows, heads=heads)
    flat = jax.ShapeDtypeStruct((rows * heads, LANES), f32)

    shards = gather_group(queries)

    local = call(
        lambda *refs: local_kernel(*refs, kv_heads=kv_heads, **sizes),
        [flat] * 3,
        [SMEM] + [VMEM] * 3,
        scratch=[pltpu.VMEM((rows * heads, HEAD_DIM), f32)],
        flops=0,
        moved=32 << 20,
    )(row_lengths, queries, cache_keys, cache_values)

    packed = call(
        lambda *refs: slot_kernel(
            *refs,
            groups=groups,
            kv_heads=kv_heads,
            slots=slots,
            chunk=math.gcd(positions, 512),
            **sizes,
        ),
        jax.ShapeDtypeStruct(((slots + 1) * heads, LANES), f32),
        [SMEM] * 3 + [VMEM] * (groups + 2) + [pl.BlockSpec(memory_space=pl.ANY)],
        scratch=[
            pltpu.VMEM((slots * heads, HEAD_DIM), f32),
            pltpu.VMEM((slots * heads, positions), f32),
        ],
        flops=0,
        moved=32 << 20,
    )(slot_owner, slot_fill, free_counts, *shards, pool_keys, pool_values, local[2])

    parts = gather_group(packed)

    block = jax.ShapeDtypeStruct((rows, columns), bf16)
    order = list(range(tp - 1, 0, -1)) + [0]
    cost = dict(flops=2 * rows * width * columns, moved=2 * width * columns)
    x, sent, free_total = call(
        lambda *refs: combine_kernel(
            *refs,
            groups=groups,
            slots=slots,
            tp_mask=order[0],
            columns=columns,
            chunk=chunk,
            **sizes,
        ),
        [
            jax.ShapeDtypeStruct((rows, width), bf16),
            block,
            jax.ShapeDtypeStruct((1,), jnp.int32),
        ],
        [VMEM] * (3 + groups + 1),
        out_specs=[VMEM, VMEM, SMEM],
        scratch=[pltpu.VMEM((rows * heads, LANES), f32)] * 3,
        **cost,
    )(*local, *parts, out_weight)
    received = [swap(sent, "tp", order[0])]
    for mask in order[1:]:
        out = call(
            lambda *refs, mask=mask: project_kernel(
                *refs, tp_mask=mask, columns=columns, chunk=chunk
            ),
            block if mask else jax.ShapeDtypeStruct((rows, columns), f32),
            [VMEM] * 2,
            **cost,
        )(x, out_weight)
        if mask:
            received.append(swap(out, "tp", mask))
    mixed_out = call(sum_kernel, block, [VMEM] * tp)(out, *received)
    return (mixed_out, free_total)


def solution(mesh):
    in_specs = (
        P("group", "tp"),
        P("group", None, "tp"),
        P("group", None, "tp"),
        P("group", None, "tp"),
        P("group", None, "tp"),
        P("group"),
        P("group"),
        P("group"),
        P("group"),
        P("tp", None),
    )
    out_specs = (P("group", "tp"), P())
    return jax.shard_map(
        per_device, mesh=mesh, in_specs=in_specs, out_specs=out_specs, check_vma=False
    )
```

```python
import math

import jax
import jax.numpy as jnp
from jax import lax
from jax.experimental import pallas as pl
from jax.experimental.pallas import tpu as pltpu
from jax.sharding import PartitionSpec as P


HEAD_DIM = 128
LANES = 128
far_below = -1e30


VMEM = pl.BlockSpec(memory_space=pltpu.VMEM)
SMEM = pl.BlockSpec(memory_space=pltpu.SMEM)
HBM = pl.BlockSpec(memory_space=pltpu.MemorySpace.HBM)
f32 = jnp.float32
bf16 = jnp.bfloat16


def call(kernel, outs, ins, scratch=(), out_specs=None, flops=0, moved=0, vmem=8 << 20):
    return pl.pallas_call(
        kernel,
        out_shape=outs,
        in_specs=ins,
        out_specs=out_specs if out_specs is not None else jax.tree.map(lambda _: VMEM, outs),
        scratch_shapes=scratch,
        cost_estimate=pl.CostEstimate(flops=flops, bytes_accessed=moved, transcendentals=0),
        compiler_params=pltpu.CompilerParams(vmem_limit_bytes=vmem),
    )


def spread_heads(tile, kv_heads):
    if kv_heads == 1:
        return tile
    heads = tile.shape[0]
    owner = lax.broadcasted_iota(jnp.int32, tile.shape, 0) // (heads // kv_heads)
    return jnp.concatenate(
        [jnp.where(owner == k, tile, jnp.zeros_like(tile)) for k in range(kv_heads)], axis=1
    )


def own_columns(wide, kv_heads):
    if kv_heads == 1:
        return wide
    heads = wide.shape[0]
    owner = lax.broadcasted_iota(jnp.int32, (heads, HEAD_DIM), 0) // (heads // kv_heads)
    picked = wide[:, :HEAD_DIM]
    for k in range(1, kv_heads):
        picked = jnp.where(owner == k, wide[:, k * HEAD_DIM : (k + 1) * HEAD_DIM], picked)
    return picked


def scores_of(query, keys):
    return lax.dot_general(
        query, keys, (((1,), (1,)), ((), ())), preferred_element_type=f32
    ) * (1.0 / math.sqrt(HEAD_DIM))


def copy_in(source, target, sem):
    copy = pltpu.make_async_copy(source, target, sem)
    copy.start()
    return copy


def local_kernel(
    lengths_in, q_in, keys_in, values_in, pool_in,
    mixed_ref, high_ref, total_ref, q_ref, pool_ref,
    lengths, keys, values, q_heads, scores, weights, sems,
    *, rows, heads, kv_heads, parts,
):
    positions = keys.shape[1]
    step = rows // parts
    lengths_copy = copy_in(lengths_in, lengths, sems.at[0])
    q_copy = copy_in(q_in, q_ref, sems.at[1])
    key_copies, value_copies = [], []
    for held, source, target, base in (
        (key_copies, keys_in, keys, 2),
        (value_copies, values_in, values, 2 + parts),
    ):
        for p in range(parts):
            at = pl.ds(p * step, step)
            held.append(copy_in(source.at[at], target.at[at], sems.at[base + p]))
    pool_copy = copy_in(pool_in, pool_ref, sems.at[2 + 2 * parts])
    q_copy.wait()
    wide = q_ref[...].astype(f32)
    for h in range(heads):
        q_heads[pl.ds(h, rows, stride=heads), :] = wide[:, h * HEAD_DIM : (h + 1) * HEAD_DIM]
    lengths_copy.wait()
    place = lax.broadcasted_iota(jnp.int32, (heads, positions), 1)
    for p in range(parts):
        key_copies[p].wait()
        for r in range(p * step, (p + 1) * step):
            at = pl.ds(r * heads, heads)
            query = spread_heads(q_heads[at, :].astype(bf16), kv_heads)
            scores[at, :] = jnp.where(place < lengths[r], scores_of(query, keys[r]), far_below)
    for r in range(rows):
        at = pl.ds(r * heads, heads)
        masked = scores[at, :]
        high = jnp.max(masked, axis=-1, keepdims=True)
        weight = jnp.where(place < lengths[r], jnp.exp(masked - high), 0.0)
        total = jnp.sum(weight, axis=-1, keepdims=True)
        weights[r] = weight.astype(bf16)
        high_ref[at, :] = jnp.broadcast_to(high, (heads, LANES))
        total_ref[at, :] = jnp.broadcast_to(total, (heads, LANES))
    for p in range(parts):
        value_copies[p].wait()
        for r in range(p * step, (p + 1) * step):
            mixed = jnp.dot(weights[r], values[r], preferred_element_type=f32)
            mixed_ref[pl.ds(r * heads, heads), :] = own_columns(mixed, kv_heads)
    pool_copy.wait()


def fetch_kernel(source, _, target, sem):
    copy_in(source, target, sem).wait()


def columns_of(weight, tp_mask, columns):
    start = jnp.bitwise_xor(lax.axis_index("tp"), tp_mask) * columns
    return weight.at[:, pl.ds(pl.multiple_of(start, columns), columns)]


def fetch_columns_kernel(source, _, target, sem, *, tp_mask, columns):
    copy_in(columns_of(source, tp_mask, columns), target, sem).wait()


def slot_kernel(*refs, groups, rows, heads, kv_heads, slots, chunk, tp_mask, columns):
    owners_in, fills_in, free = refs[:3]
    shards = refs[3 : 3 + groups]
    keys, values, weight_in = refs[3 + groups : 6 + groups]
    packed, weight, owners, fills, q_heads, scores, sems = refs[6 + groups :]
    copies = [
        copy_in(owners_in, owners, sems.at[0]),
        copy_in(fills_in, fills, sems.at[1]),
    ]
    weight_copy = copy_in(columns_of(weight_in, tp_mask, columns), weight, sems.at[2])
    for copy in copies:
        copy.wait()
    positions = keys.shape[1]
    me = lax.axis_index("group")
    row_at = lax.broadcasted_iota(jnp.int32, (rows, heads * HEAD_DIM), 0)
    for s in range(slots):
        owner = jnp.maximum(owners[s], 0)
        home = lax.div(owner, rows)
        row = lax.rem(owner, rows)
        for k in range(groups):

            @pl.when(jnp.bitwise_xor(home, me) == k)
            def _(k=k, s=s, row=row):
                block = jnp.where(row_at == row, shards[k][...].astype(f32), 0.0)
                single = jnp.sum(block, axis=0, keepdims=True)
                for h in range(heads):
                    q_heads[s * heads + h : s * heads + h + 1, :] = single[
                        :, h * HEAD_DIM : (h + 1) * HEAD_DIM
                    ]

    place = lax.broadcasted_iota(jnp.int32, (heads, positions), 1)
    lane = lax.broadcasted_iota(jnp.int32, (heads, LANES), 1)
    stats = jnp.where(lane == 3 * slots, free[0].astype(f32), 0.0)
    for s in range(slots):
        at = pl.ds(s * heads, heads)
        query = spread_heads(q_heads[at, :].astype(bf16), kv_heads)
        for c in range(0, positions, chunk):
            scores[at, c : c + chunk] = scores_of(query, keys[s, c : c + chunk, :])
    for s in range(slots):
        at = pl.ds(s * heads, heads)
        visible = place < fills[s]
        masked = jnp.where(visible, scores[at, :], far_below)
        high = jnp.max(masked, axis=-1, keepdims=True)
        weights = jnp.where(visible, jnp.exp(masked - high), 0.0)
        total = jnp.sum(weights, axis=-1, keepdims=True)
        mixed = jnp.dot(weights.astype(bf16), values[s], preferred_element_type=f32)
        packed[at, :] = own_columns(mixed, kv_heads)
        stats = jnp.where(lane == s, high, stats)
        stats = jnp.where(lane == slots + s, total, stats)
        stats = jnp.where(lane == 2 * slots + s, owners[s].astype(f32), stats)
    packed[slots * heads :, :] = stats
    weight_copy.wait()


def project(x, weight, out, chunk):
    for c in range(0, out.shape[1], chunk):
        out[:, c : c + chunk] = jnp.dot(
            x, weight[:, c : c + chunk], preferred_element_type=f32
        ).astype(out.dtype)


def combine_kernel(*refs, groups, rows, heads, slots, ahead, columns, chunk):
    mixed_ref, high_ref, total_ref = refs[:3]
    parts = refs[3 : 3 + groups]
    weight, weight_in, x_ref, out, free_total = refs[3 + groups : 8 + groups]
    rest = refs[8 + groups :]
    copy = None
    if ahead is not None:
        copy = copy_in(columns_of(weight_in, ahead, columns), rest[0], rest[-1])
        rest = rest[1:-1]
    mixed, high, total = rest
    first = lax.axis_index("group") * rows
    free = jnp.zeros((heads, LANES), f32)
    found = []
    for k in range(groups):
        stats = parts[k][slots * heads :, :]
        free = free + stats
        for s in range(slots):
            row = stats[0, 2 * slots + s].astype(jnp.int32) - first
            found.append((k, s, row))
    free_total[0] = free[0, 3 * slots].astype(jnp.int32)
    high[...] = high_ref[...]
    slot_stats = []
    for k, s, row in found:
        mine = (row >= 0) & (row < rows)
        at = pl.ds(pl.multiple_of(jnp.clip(row, 0, rows - 1) * heads, heads), heads)
        stats = parts[k][slots * heads :, :]
        slot_high = jnp.broadcast_to(stats[:, s : s + 1], (heads, LANES))
        slot_total = jnp.broadcast_to(stats[:, slots + s : slots + s + 1], (heads, LANES))
        slot_stats.append((mine, at, slot_high, slot_total))
        high[at, :] = jnp.maximum(high[at, :], jnp.where(mine, slot_high, far_below))
    keep = jnp.exp(high_ref[...] - high[...])
    mixed[...] = keep * mixed_ref[...]
    total[...] = keep * total_ref[...]
    for (k, s, _), (mine, at, slot_high, slot_total) in zip(found, slot_stats):
        add = jnp.where(mine, jnp.exp(jnp.minimum(slot_high - high[at, :], 0.0)), 0.0)
        mixed[at, :] = mixed[at, :] + add * parts[k][s * heads : (s + 1) * heads, :]
        total[at, :] = total[at, :] + add * slot_total
    mixed[...] = mixed[...] / total[...]
    for h in range(heads):
        x_ref[:, h * HEAD_DIM : (h + 1) * HEAD_DIM] = mixed[
            pl.ds(h, rows, stride=heads), :
        ].astype(bf16)
    project(x_ref[...], weight, out, chunk)
    if copy is not None:
        copy.wait()


def project_kernel(x_ref, weight, weight_in, out, *rest, ahead, columns, chunk):
    copy = None
    if ahead is not None:
        copy = copy_in(columns_of(weight_in, ahead, columns), *rest)
    project(x_ref[...], weight, out, chunk)
    if copy is not None:
        copy.wait()


def sum_kernel(*refs):
    total = refs[0][...]
    for part in refs[1:-1]:
        total = total + part[...].astype(f32)
    refs[-1][...] = total.astype(bf16)


def swap(value, axis, mask):
    size = lax.axis_size(axis)
    return lax.ppermute(value, axis, [(i, i ^ mask) for i in range(size)])


def gather_group(value):
    groups = lax.axis_size("group")
    found = [None] * groups
    found[0] = value
    found[1] = swap(value, "group", 1)
    for k in range(2, groups, 2):
        found[k] = swap(value, "group", k)
    for k in range(2, groups, 2):
        found[k + 1] = swap(found[k], "group", 1)
    return found


def step(
    queries,
    cache_keys,
    cache_values,
    pool_keys,
    pool_values,
    row_lengths,
    slot_owner,
    slot_fill,
    free_counts,
    out_weight,
):
    groups, tp = lax.axis_size("group"), lax.axis_size("tp")
    rows, width = queries.shape
    heads = width // HEAD_DIM
    kv_heads = cache_keys.shape[2] // HEAD_DIM
    slots, positions = pool_keys.shape[:2]
    columns = out_weight.shape[1] // tp
    chunk = math.gcd(columns, 512)
    sizes = dict(rows=rows, heads=heads)
    flat = jax.ShapeDtypeStruct((rows * heads, LANES), f32)

    parts = math.gcd(rows, 4)
    shards = gather_group(queries)
    (
        queries, cache_keys, cache_values, pool_keys, pool_values,
        row_lengths, slot_owner, slot_fill, out_weight,
    ) = (
        pltpu.with_memory_space_constraint(argument, pltpu.MemorySpace.HBM)
        for argument in (
            queries, cache_keys, cache_values, pool_keys, pool_values,
            row_lengths, slot_owner, slot_fill, out_weight,
        )
    )
    copies = pltpu.SemaphoreType.DMA

    *local, own_queries, held_keys = call(
        lambda *refs: local_kernel(*refs, kv_heads=kv_heads, parts=parts, **sizes),
        [flat] * 3
        + [
            jax.ShapeDtypeStruct(queries.shape, queries.dtype),
            jax.ShapeDtypeStruct(pool_keys.shape, pool_keys.dtype),
        ],
        [HBM] * 5,
        scratch=[
            pltpu.SMEM(row_lengths.shape, jnp.int32),
            pltpu.VMEM(cache_keys.shape, bf16),
            pltpu.VMEM(cache_values.shape, bf16),
            pltpu.VMEM((rows * heads, HEAD_DIM), f32),
            pltpu.VMEM((rows * heads, cache_keys.shape[1]), f32),
            pltpu.VMEM((rows, heads, cache_keys.shape[1]), bf16),
            copies((3 + 2 * parts,)),
        ],
        moved=2 * (cache_keys.size + cache_values.size + pool_keys.size),
        vmem=12 << 20,
    )(row_lengths, queries, cache_keys, cache_values, pool_keys)
    shards[0] = own_queries

    held_values = call(
        fetch_kernel,
        jax.ShapeDtypeStruct(pool_values.shape, pool_values.dtype),
        [HBM, pl.BlockSpec(memory_space=pl.ANY)],
        scratch=[copies],
        moved=2 * pool_values.size,
        vmem=1 << 20,
    )(pool_values, own_queries)

    order = list(range(tp - 1, 0, -1)) + [0]
    held = jax.ShapeDtypeStruct((width, columns), out_weight.dtype)
    weights = {}
    packed, weights[order[0]] = call(
        lambda *refs: slot_kernel(
            *refs,
            groups=groups,
            kv_heads=kv_heads,
            slots=slots,
            chunk=math.gcd(positions, 512),
            tp_mask=order[0],
            columns=columns,
            **sizes,
        ),
        [jax.ShapeDtypeStruct(((slots + 1) * heads, LANES), f32), held],
        [HBM] * 2 + [SMEM] + [VMEM] * (groups + 2) + [HBM],
        scratch=[
            pltpu.SMEM(slot_owner.shape, jnp.int32),
            pltpu.SMEM(slot_fill.shape, jnp.int32),
            pltpu.VMEM((slots * heads, HEAD_DIM), f32),
            pltpu.VMEM((slots * heads, positions), f32),
            copies((3,)),
        ],
        moved=2 * width * columns,
        vmem=8 << 20,
    )(slot_owner, slot_fill, free_counts, *shards, held_keys, held_values, out_weight)

    far = gather_group(packed)

    if tp > 1:
        weights[order[1]] = call(
            lambda *refs: fetch_columns_kernel(*refs, tp_mask=order[1], columns=columns),
            held,
            [HBM, pl.BlockSpec(memory_space=pl.ANY)],
            scratch=[copies],
            moved=2 * width * columns,
            vmem=1 << 20,
        )(out_weight, packed)

    block = jax.ShapeDtypeStruct((rows, columns), bf16)
    whole = jax.ShapeDtypeStruct((rows, columns), f32)
    moved = 2 * width * columns
    ahead = order[2] if tp > 2 else None
    x, sent, free_total, *more = call(
        lambda *refs: combine_kernel(
            *refs, groups=groups, slots=slots, ahead=ahead, columns=columns, chunk=chunk, **sizes
        ),
        [
            jax.ShapeDtypeStruct((rows, width), bf16),
            block if tp > 1 else whole,
            jax.ShapeDtypeStruct((1,), jnp.int32),
        ]
        + [held] * (ahead is not None),
        [VMEM] * (3 + groups + 1) + [HBM],
        out_specs=[VMEM, VMEM, SMEM] + [VMEM] * (ahead is not None),
        scratch=[pltpu.VMEM((rows * heads, LANES), f32)] * 3 + [copies] * (ahead is not None),
        moved=moved,
    )(*local, *far, weights[order[0]], out_weight)
    out = sent
    received = []
    for i in range(1, tp):
        received.append(swap(sent, "tp", order[i - 1]))
        if more:
            weights[order[i + 1]] = more[0]
        ahead = order[i + 2] if i + 2 < tp else None
        sent, *more = call(
            lambda *refs, ahead=ahead: project_kernel(
                *refs, ahead=ahead, columns=columns, chunk=chunk
            ),
            [block if order[i] else whole] + [held] * (ahead is not None),
            [VMEM] * 2 + [HBM],
            scratch=[copies] * (ahead is not None),
            moved=moved,
            vmem=4 << 20,
        )(x, weights[order[i]], out_weight)
    out = sent
    mixed_out = call(sum_kernel, block, [VMEM] * tp)(out, *received)
    return (mixed_out, free_total)


def solution(mesh):
    in_specs = (
        P("group", "tp"),
        P("group", None, "tp"),
        P("group", None, "tp"),
        P("group", None, "tp"),
        P("group", None, "tp"),
        P("group"),
        P("group"),
        P("group"),
        P("group"),
        P("tp", None),
    )
    out_specs = (P("group", "tp"), P())
    return jax.shard_map(step, mesh=mesh, in_specs=in_specs, out_specs=out_specs, check_vma=False)
```

```python
import math

import jax
import jax.numpy as jnp
from jax import lax
from jax.experimental import pallas as pl
from jax.experimental.pallas import tpu as pltpu
from jax.sharding import PartitionSpec as P


HEAD_DIM = 128
LANES = 128
far_below = -1e30


VMEM = pl.BlockSpec(memory_space=pltpu.VMEM)
SMEM = pl.BlockSpec(memory_space=pltpu.SMEM)
HBM = pl.BlockSpec(memory_space=pltpu.MemorySpace.HBM)
f32 = jnp.float32
bf16 = jnp.bfloat16


def call(kernel, outs, ins, scratch=(), out_specs=None, flops=0, moved=0, vmem=8 << 20):
    return pl.pallas_call(
        kernel,
        out_shape=outs,
        in_specs=ins,
        out_specs=out_specs if out_specs is not None else jax.tree.map(lambda _: VMEM, outs),
        scratch_shapes=scratch,
        cost_estimate=pl.CostEstimate(flops=flops, bytes_accessed=moved, transcendentals=0),
        compiler_params=pltpu.CompilerParams(vmem_limit_bytes=vmem),
    )


def spread_heads(tile, kv_heads):
    if kv_heads == 1:
        return tile
    heads = tile.shape[0]
    owner = lax.broadcasted_iota(jnp.int32, tile.shape, 0) // (heads // kv_heads)
    return jnp.concatenate(
        [jnp.where(owner == k, tile, jnp.zeros_like(tile)) for k in range(kv_heads)], axis=1
    )


def own_columns(wide, kv_heads):
    if kv_heads == 1:
        return wide
    heads = wide.shape[0]
    owner = lax.broadcasted_iota(jnp.int32, (heads, HEAD_DIM), 0) // (heads // kv_heads)
    picked = wide[:, :HEAD_DIM]
    for k in range(1, kv_heads):
        picked = jnp.where(owner == k, wide[:, k * HEAD_DIM : (k + 1) * HEAD_DIM], picked)
    return picked


def scores_of(query, keys):
    return lax.dot_general(
        query, keys, (((1,), (1,)), ((), ())), preferred_element_type=f32
    ) * (1.0 / math.sqrt(HEAD_DIM))


def copy_in(source, target, sem):
    copy = pltpu.make_async_copy(source, target, sem)
    copy.start()
    return copy


def local_kernel(
    lengths_in, q_in, keys_in, values_in, pool_in,
    packed, q_ref, pool_ref,
    lengths, keys, values, q_heads, scores, weights, sems,
    *, rows, heads, kv_heads, parts,
):
    positions = keys.shape[1]
    step = rows // parts
    lengths_copy = copy_in(lengths_in, lengths, sems.at[0])
    q_copy = copy_in(q_in, q_ref, sems.at[1])
    key_copies, value_copies = [], []
    for held, source, target, base in (
        (key_copies, keys_in, keys, 2),
        (value_copies, values_in, values, 2 + parts),
    ):
        for p in range(parts):
            at = pl.ds(p * step, step)
            held.append(copy_in(source.at[at], target.at[at], sems.at[base + p]))
    pool_copy = copy_in(pool_in, pool_ref, sems.at[2 + 2 * parts])
    q_copy.wait()
    wide = q_ref[...].astype(f32)
    for h in range(heads):
        q_heads[pl.ds(h, rows, stride=heads), :] = wide[:, h * HEAD_DIM : (h + 1) * HEAD_DIM]
    lengths_copy.wait()
    place = lax.broadcasted_iota(jnp.int32, (heads, positions), 1)
    lane = lax.broadcasted_iota(jnp.int32, (heads, LANES), 1)
    for p in range(parts):
        key_copies[p].wait()
        for r in range(p * step, (p + 1) * step):
            at = pl.ds(r * heads, heads)
            query = spread_heads(q_heads[at, :].astype(bf16), kv_heads)
            scores[at, :] = jnp.where(place < lengths[r], scores_of(query, keys[r]), far_below)
    for r in range(rows):
        at = pl.ds(r * heads, heads)
        masked = scores[at, :]
        high = jnp.max(masked, axis=-1, keepdims=True)
        weight = jnp.where(place < lengths[r], jnp.exp(masked - high), 0.0)
        total = jnp.sum(weight, axis=-1, keepdims=True)
        weights[r] = weight.astype(bf16)
        packed[pl.ds((rows + r) * heads, heads), :] = jnp.where(lane == 0, high, total)
    for p in range(parts):
        value_copies[p].wait()
        for r in range(p * step, (p + 1) * step):
            mixed = jnp.dot(weights[r], values[r], preferred_element_type=f32)
            packed[pl.ds(r * heads, heads), :] = own_columns(mixed, kv_heads)
    pool_copy.wait()


def fetch_kernel(source, _, target, sem):
    copy_in(source, target, sem).wait()


def step_mask(group, step, tp):
    return (tp // 2) * (group % 2) + step


def columns_of(weight, step, columns):
    tp = lax.axis_size("tp")
    mask = step_mask(lax.axis_index("group"), step, tp)
    start = jnp.bitwise_xor(lax.axis_index("tp"), mask) * columns
    return weight.at[:, pl.ds(pl.multiple_of(start, columns), columns)]


def fetch_columns_kernel(source, _, target, sem, *, step, columns):
    copy_in(columns_of(source, step, columns), target, sem).wait()


def slot_kernel(*refs, groups, rows, heads, kv_heads, slots, chunk, step, columns):
    owners_in, fills_in, free = refs[:3]
    shards = refs[3 : 3 + groups]
    keys, values, weight_in = refs[3 + groups : 6 + groups]
    packed, weight, owners, fills, q_heads, scores, sems = refs[6 + groups :]
    copies = [
        copy_in(owners_in, owners, sems.at[0]),
        copy_in(fills_in, fills, sems.at[1]),
    ]
    weight_copy = copy_in(columns_of(weight_in, step, columns), weight, sems.at[2])
    for copy in copies:
        copy.wait()
    positions = keys.shape[1]
    me = lax.axis_index("group")
    row_at = lax.broadcasted_iota(jnp.int32, (rows, heads * HEAD_DIM), 0)
    for s in range(slots):
        owner = jnp.maximum(owners[s], 0)
        home = lax.div(owner, rows)
        row = lax.rem(owner, rows)
        for k in range(groups):

            @pl.when(jnp.bitwise_xor(home, me) == k)
            def _(k=k, s=s, row=row):
                block = jnp.where(row_at == row, shards[k][...].astype(f32), 0.0)
                single = jnp.sum(block, axis=0, keepdims=True)
                for h in range(heads):
                    q_heads[s * heads + h : s * heads + h + 1, :] = single[
                        :, h * HEAD_DIM : (h + 1) * HEAD_DIM
                    ]

    place = lax.broadcasted_iota(jnp.int32, (heads, positions), 1)
    lane = lax.broadcasted_iota(jnp.int32, (heads, LANES), 1)
    stats = jnp.where(lane == 3 * slots, free[0].astype(f32), 0.0)
    for s in range(slots):
        at = pl.ds(s * heads, heads)
        query = spread_heads(q_heads[at, :].astype(bf16), kv_heads)
        for c in range(0, positions, chunk):
            scores[at, c : c + chunk] = scores_of(query, keys[s, c : c + chunk, :])
    for s in range(slots):
        at = pl.ds(s * heads, heads)
        visible = place < fills[s]
        masked = jnp.where(visible, scores[at, :], far_below)
        high = jnp.max(masked, axis=-1, keepdims=True)
        weights = jnp.where(visible, jnp.exp(masked - high), 0.0)
        total = jnp.sum(weights, axis=-1, keepdims=True)
        mixed = jnp.dot(weights.astype(bf16), values[s], preferred_element_type=f32)
        packed[at, :] = own_columns(mixed, kv_heads)
        stats = jnp.where(lane == s, high, stats)
        stats = jnp.where(lane == slots + s, total, stats)
        stats = jnp.where(lane == 2 * slots + s, owners[s].astype(f32), stats)
    packed[slots * heads :, :] = stats
    weight_copy.wait()


def project(x, weight, same, other, chunk, own=None):
    rows = x.shape[0] // 2
    for c in range(0, same.shape[1], chunk):
        product = jnp.dot(x, weight[:, c : c + chunk], preferred_element_type=f32)
        same[:, c : c + chunk] = product[:rows].astype(same.dtype)
        other[:, c : c + chunk] = product[rows:].astype(other.dtype)
        if own is not None:
            own[:, c : c + chunk] = product[:rows]


def combine_kernel(*refs, groups, rows, heads, slots, ahead, last, columns, chunk):
    local = refs[:2]
    parts = refs[2 : 2 + groups]
    weight, weight_in, x_ref, free_total, same, other = refs[2 + groups : 8 + groups]
    rest = list(refs[8 + groups :])
    own = rest.pop(0) if last else None
    copy = None
    if ahead is not None:
        copy = copy_in(columns_of(weight_in, ahead, columns), rest.pop(0), rest.pop())
    mixed, high, total = rest
    flat = rows * heads
    me = lax.axis_index("group")
    first, second = me * rows, jnp.bitwise_xor(me, 1) * rows
    free = jnp.zeros((heads, LANES), f32)
    found = []
    for k in range(groups):
        stats = parts[k][slots * heads :, :]
        free = free + stats
        for s in range(slots):
            owner = stats[0, 2 * slots + s].astype(jnp.int32)
            found.append((k, s, owner))
    free_total[0] = free[0, 3 * slots].astype(jnp.int32)
    for i in range(2):
        stats = local[i][flat:, :]
        high[i * flat : (i + 1) * flat, :] = jnp.broadcast_to(stats[:, 0:1], (flat, LANES))
    slot_stats = []
    for k, s, owner in found:
        in_first = (owner >= first) & (owner < first + rows)
        in_second = (owner >= second) & (owner < second + rows)
        row = jnp.where(
            in_first, owner - first, jnp.where(in_second, owner - second + rows, 0)
        )
        mine = in_first | in_second
        at = pl.ds(pl.multiple_of(row * heads, heads), heads)
        stats = parts[k][slots * heads :, :]
        slot_high = jnp.broadcast_to(stats[:, s : s + 1], (heads, LANES))
        slot_total = jnp.broadcast_to(stats[:, slots + s : slots + s + 1], (heads, LANES))
        slot_stats.append((mine, at, slot_high, slot_total))
        high[at, :] = jnp.maximum(high[at, :], jnp.where(mine, slot_high, far_below))
    for i in range(2):
        at = slice(i * flat, (i + 1) * flat)
        stats = local[i][flat:, :]
        keep = jnp.exp(jnp.broadcast_to(stats[:, 0:1], (flat, LANES)) - high[at, :])
        mixed[at, :] = keep * local[i][:flat, :]
        total[at, :] = keep * jnp.broadcast_to(stats[:, 1:2], (flat, LANES))
    for (k, s, _), (mine, at, slot_high, slot_total) in zip(found, slot_stats):
        add = jnp.where(mine, jnp.exp(jnp.minimum(slot_high - high[at, :], 0.0)), 0.0)
        mixed[at, :] = mixed[at, :] + add * parts[k][s * heads : (s + 1) * heads, :]
        total[at, :] = total[at, :] + add * slot_total
    mixed[...] = mixed[...] / total[...]
    for h in range(heads):
        x_ref[:, h * HEAD_DIM : (h + 1) * HEAD_DIM] = mixed[
            pl.ds(h, 2 * rows, stride=heads), :
        ].astype(bf16)
    project(x_ref[...], weight, same, other, chunk, own)
    if copy is not None:
        copy.wait()


def project_kernel(x_ref, weight, weight_in, same, other, *rest, ahead, last, columns, chunk):
    rest = list(rest)
    own = rest.pop(0) if last else None
    copy = None
    if ahead is not None:
        copy = copy_in(columns_of(weight_in, ahead, columns), *rest)
    project(x_ref[...], weight, same, other, chunk, own)
    if copy is not None:
        copy.wait()


def sum_kernel(own, final, *refs):
    total = jnp.where(lax.axis_index("group") % 2 == 0, own[...], final[...].astype(f32))
    for part in refs[:-1]:
        total = total + part[...].astype(f32)
    refs[-1][...] = total.astype(bf16)


def send_block(value, step, cross):
    groups, tp = lax.axis_size("group"), lax.axis_size("tp")
    pairs = [
        (g * tp + z, (g ^ cross) * tp + (z ^ step_mask(g, step, tp)))
        for g in range(groups)
        for z in range(tp)
        if cross or step_mask(g, step, tp)
    ]
    return lax.ppermute(value, ("group", "tp"), pairs)


def swap(value, axis, mask):
    size = lax.axis_size(axis)
    return lax.ppermute(value, axis, [(i, i ^ mask) for i in range(size)])


def gather_group(value):
    groups = lax.axis_size("group")
    found = [None] * groups
    found[0] = value
    found[1] = swap(value, "group", 1)
    for k in range(2, groups, 2):
        found[k] = swap(value, "group", k)
    for k in range(2, groups, 2):
        found[k + 1] = swap(found[k], "group", 1)
    return found


def step(
    queries,
    cache_keys,
    cache_values,
    pool_keys,
    pool_values,
    row_lengths,
    slot_owner,
    slot_fill,
    free_counts,
    out_weight,
):
    groups, tp = lax.axis_size("group"), lax.axis_size("tp")
    rows, width = queries.shape
    heads = width // HEAD_DIM
    kv_heads = cache_keys.shape[2] // HEAD_DIM
    slots, positions = pool_keys.shape[:2]
    columns = out_weight.shape[1] // tp
    chunk = math.gcd(columns, 512)
    sizes = dict(rows=rows, heads=heads)

    parts = math.gcd(rows, 4)
    shards = gather_group(queries)
    (
        queries, cache_keys, cache_values, pool_keys, pool_values,
        row_lengths, slot_owner, slot_fill, out_weight,
    ) = (
        pltpu.with_memory_space_constraint(argument, pltpu.MemorySpace.HBM)
        for argument in (
            queries, cache_keys, cache_values, pool_keys, pool_values,
            row_lengths, slot_owner, slot_fill, out_weight,
        )
    )
    copies = pltpu.SemaphoreType.DMA

    local, own_queries, held_keys = call(
        lambda *refs: local_kernel(*refs, kv_heads=kv_heads, parts=parts, **sizes),
        [
            jax.ShapeDtypeStruct((2 * rows * heads, LANES), f32),
            jax.ShapeDtypeStruct(queries.shape, queries.dtype),
            jax.ShapeDtypeStruct(pool_keys.shape, pool_keys.dtype),
        ],
        [HBM] * 5,
        scratch=[
            pltpu.SMEM(row_lengths.shape, jnp.int32),
            pltpu.VMEM(cache_keys.shape, bf16),
            pltpu.VMEM(cache_values.shape, bf16),
            pltpu.VMEM((rows * heads, HEAD_DIM), f32),
            pltpu.VMEM((rows * heads, cache_keys.shape[1]), f32),
            pltpu.VMEM((rows, heads, cache_keys.shape[1]), bf16),
            copies((3 + 2 * parts,)),
        ],
        moved=2 * (cache_keys.size + cache_values.size + pool_keys.size),
        vmem=12 << 20,
    )(row_lengths, queries, cache_keys, cache_values, pool_keys)
    shards[0] = own_queries
    pair_local = swap(local, "group", 1)

    held_values = call(
        fetch_kernel,
        jax.ShapeDtypeStruct(pool_values.shape, pool_values.dtype),
        [HBM, pl.BlockSpec(memory_space=pl.ANY)],
        scratch=[copies],
        moved=2 * pool_values.size,
        vmem=1 << 20,
    )(pool_values, own_queries)

    order = list(range(tp // 2 - 1, -1, -1))
    held = jax.ShapeDtypeStruct((width, columns), out_weight.dtype)
    weights = {}
    packed, weights[order[0]] = call(
        lambda *refs: slot_kernel(
            *refs,
            groups=groups,
            kv_heads=kv_heads,
            slots=slots,
            chunk=math.gcd(positions, 512),
            step=order[0],
            columns=columns,
            **sizes,
        ),
        [jax.ShapeDtypeStruct(((slots + 1) * heads, LANES), f32), held],
        [HBM] * 2 + [SMEM] + [VMEM] * (groups + 2) + [HBM],
        scratch=[
            pltpu.SMEM(slot_owner.shape, jnp.int32),
            pltpu.SMEM(slot_fill.shape, jnp.int32),
            pltpu.VMEM((slots * heads, HEAD_DIM), f32),
            pltpu.VMEM((slots * heads, positions), f32),
            copies((3,)),
        ],
        moved=2 * width * columns,
        vmem=8 << 20,
    )(slot_owner, slot_fill, free_counts, *shards, held_keys, held_values, out_weight)

    far = gather_group(packed)

    if len(order) > 1:
        weights[order[1]] = call(
            lambda *refs: fetch_columns_kernel(*refs, step=order[1], columns=columns),
            held,
            [HBM, pl.BlockSpec(memory_space=pl.ANY)],
            scratch=[copies],
            moved=2 * width * columns,
            vmem=1 << 20,
        )(out_weight, packed)

    block = jax.ShapeDtypeStruct((rows, columns), bf16)
    whole = jax.ShapeDtypeStruct((rows, columns), f32)
    moved = 2 * width * columns
    received = []
    for i, step in enumerate(order):
        last = step == 0
        ahead = order[i + 2] if i + 2 < len(order) else None
        outs = [block] * 2 + [whole] * last + [held] * (ahead is not None)
        settings = dict(ahead=ahead, last=last, columns=columns, chunk=chunk)
        if i == 0:
            x, free_total, same, other, *more = call(
                lambda *refs: combine_kernel(
                    *refs, groups=groups, slots=slots, **settings, **sizes
                ),
                [
                    jax.ShapeDtypeStruct((2 * rows, width), bf16),
                    jax.ShapeDtypeStruct((1,), jnp.int32),
                ]
                + outs,
                [VMEM] * (2 + groups + 1) + [HBM],
                out_specs=[VMEM, SMEM] + [VMEM] * len(outs),
                scratch=[pltpu.VMEM((2 * rows * heads, LANES), f32)] * 3
                + [copies] * (ahead is not None),
                moved=moved,
            )(local, pair_local, *far, weights[step], out_weight)
        else:
            same, other, *more = call(
                lambda *refs, settings=settings: project_kernel(*refs, **settings),
                outs,
                [VMEM] * 2 + [HBM],
                scratch=[copies] * (ahead is not None),
                moved=moved,
                vmem=4 << 20,
            )(x, weights[step], out_weight)
        if last:
            own = more.pop(0)
        if ahead is not None:
            weights[ahead] = more.pop(0)
        received.append(send_block(same, step, 0))
        received.append(send_block(other, step, 1))
    final = received.pop(-2)
    mixed_out = call(sum_kernel, block, [VMEM] * (2 + len(received)))(
        own, final, *received
    )
    return (mixed_out, free_total)


def solution(mesh):
    in_specs = (
        P("group", "tp"),
        P("group", None, "tp"),
        P("group", None, "tp"),
        P("group", None, "tp"),
        P("group", None, "tp"),
        P("group"),
        P("group"),
        P("group"),
        P("group"),
        P("tp", None),
    )
    out_specs = (P("group", "tp"), P())
    return jax.shard_map(step, mesh=mesh, in_specs=in_specs, out_specs=out_specs, check_vma=False)
```

```python
import math

import jax
import jax.numpy as jnp
from jax import lax
from jax.experimental import pallas as pl
from jax.experimental.pallas import tpu as pltpu
from jax.sharding import PartitionSpec as P


HEAD_DIM = 128
LANES = 128
far_below = -1e30


VMEM = pl.BlockSpec(memory_space=pltpu.VMEM)
SMEM = pl.BlockSpec(memory_space=pltpu.SMEM)
HBM = pl.BlockSpec(memory_space=pltpu.MemorySpace.HBM)
f32 = jnp.float32
bf16 = jnp.bfloat16


def call(kernel, outs, ins, scratch=(), out_specs=None, flops=0, moved=0, vmem=8 << 20):
    return pl.pallas_call(
        kernel,
        out_shape=outs,
        in_specs=ins,
        out_specs=out_specs if out_specs is not None else jax.tree.map(lambda _: VMEM, outs),
        scratch_shapes=scratch,
        cost_estimate=pl.CostEstimate(flops=flops, bytes_accessed=moved, transcendentals=0),
        compiler_params=pltpu.CompilerParams(vmem_limit_bytes=vmem),
    )


def spread_heads(tile, kv_heads):
    if kv_heads == 1:
        return tile
    heads = tile.shape[0]
    owner = lax.broadcasted_iota(jnp.int32, tile.shape, 0) // (heads // kv_heads)
    return jnp.concatenate(
        [jnp.where(owner == k, tile, jnp.zeros_like(tile)) for k in range(kv_heads)], axis=1
    )


def own_columns(wide, kv_heads):
    if kv_heads == 1:
        return wide
    heads = wide.shape[0]
    owner = lax.broadcasted_iota(jnp.int32, (heads, HEAD_DIM), 0) // (heads // kv_heads)
    picked = wide[:, :HEAD_DIM]
    for k in range(1, kv_heads):
        picked = jnp.where(owner == k, wide[:, k * HEAD_DIM : (k + 1) * HEAD_DIM], picked)
    return picked


def scores_of(query, keys):
    return lax.dot_general(
        query, keys, (((1,), (1,)), ((), ())), preferred_element_type=f32
    ) * (1.0 / math.sqrt(HEAD_DIM))


def copy_in(source, target, sem):
    copy = pltpu.make_async_copy(source, target, sem)
    copy.start()
    return copy


def open_kernel(_, token):
    token[...] = jnp.zeros_like(token)


def local_kernel(
    lengths_in, q_in, keys, values, weight_in, _,
    packed, q_ref, weight,
    lengths, q_heads, scores, weights, sems,
    *, rows, heads, kv_heads, step, columns,
):
    positions = keys.shape[1]
    lengths_copy = copy_in(lengths_in, lengths, sems.at[0])
    q_copy = copy_in(q_in, q_ref, sems.at[1])
    weight_copy = copy_in(columns_of(weight_in, step, columns), weight, sems.at[2])
    q_copy.wait()
    wide = q_ref[...].astype(f32)
    for h in range(heads):
        q_heads[pl.ds(h, rows, stride=heads), :] = wide[:, h * HEAD_DIM : (h + 1) * HEAD_DIM]
    lengths_copy.wait()
    place = lax.broadcasted_iota(jnp.int32, (heads, positions), 1)
    lane = lax.broadcasted_iota(jnp.int32, (heads, LANES), 1)
    for r in range(rows):
        at = pl.ds(r * heads, heads)
        query = spread_heads(q_heads[at, :].astype(bf16), kv_heads)
        scores[at, :] = jnp.where(place < lengths[r], scores_of(query, keys[r]), far_below)
    for r in range(rows):
        at = pl.ds(r * heads, heads)
        masked = scores[at, :]
        high = jnp.max(masked, axis=-1, keepdims=True)
        weight_of = jnp.where(place < lengths[r], jnp.exp(masked - high), 0.0)
        total = jnp.sum(weight_of, axis=-1, keepdims=True)
        weights[r] = weight_of.astype(bf16)
        packed[pl.ds((rows + r) * heads, heads), :] = jnp.where(lane == 0, high, total)
    for r in range(rows):
        mixed = jnp.dot(weights[r], values[r], preferred_element_type=f32)
        packed[pl.ds(r * heads, heads), :] = own_columns(mixed, kv_heads)
    weight_copy.wait()


def step_mask(group, step):
    return 2 * step + group % 2


def columns_of(weight, step, columns):
    mask = step_mask(lax.axis_index("group"), step)
    start = jnp.bitwise_xor(lax.axis_index("tp"), mask) * columns
    return weight.at[:, pl.ds(pl.multiple_of(start, columns), columns)]


def slot_kernel(*refs, groups, rows, heads, kv_heads, slots, chunk, ahead, columns):
    owners_in, fills_in, free = refs[:3]
    shards = refs[3 : 3 + groups]
    keys, values, weight_in = refs[3 + groups : 6 + groups]
    packed, *rest = refs[6 + groups :]
    weight_copy = None
    if ahead is not None:
        weight_copy = copy_in(columns_of(weight_in, ahead, columns), rest[0], rest[-1].at[2])
        rest = rest[1:]
    owners, fills, q_heads, scores, sems = rest
    copies = [
        copy_in(owners_in, owners, sems.at[0]),
        copy_in(fills_in, fills, sems.at[1]),
    ]
    for copy in copies:
        copy.wait()
    positions = keys.shape[1]
    me = lax.axis_index("group")
    row_at = lax.broadcasted_iota(jnp.int32, (rows, heads * HEAD_DIM), 0)
    for s in range(slots):
        owner = jnp.maximum(owners[s], 0)
        home = lax.div(owner, rows)
        row = lax.rem(owner, rows)
        for k in range(groups):

            @pl.when(jnp.bitwise_xor(home, me) == k)
            def _(k=k, s=s, row=row):
                block = jnp.where(row_at == row, shards[k][...].astype(f32), 0.0)
                single = jnp.sum(block, axis=0, keepdims=True)
                for h in range(heads):
                    q_heads[s * heads + h : s * heads + h + 1, :] = single[
                        :, h * HEAD_DIM : (h + 1) * HEAD_DIM
                    ]

    place = lax.broadcasted_iota(jnp.int32, (heads, positions), 1)
    lane = lax.broadcasted_iota(jnp.int32, (heads, LANES), 1)
    stats = jnp.where(lane == 3 * slots, free[0].astype(f32), 0.0)
    for s in range(slots):
        at = pl.ds(s * heads, heads)
        query = spread_heads(q_heads[at, :].astype(bf16), kv_heads)
        for c in range(0, positions, chunk):
            scores[at, c : c + chunk] = scores_of(query, keys[s, c : c + chunk, :])
    for s in range(slots):
        at = pl.ds(s * heads, heads)
        visible = place < fills[s]
        masked = jnp.where(visible, scores[at, :], far_below)
        high = jnp.max(masked, axis=-1, keepdims=True)
        weights = jnp.where(visible, jnp.exp(masked - high), 0.0)
        total = jnp.sum(weights, axis=-1, keepdims=True)
        mixed = jnp.dot(weights.astype(bf16), values[s], preferred_element_type=f32)
        packed[at, :] = own_columns(mixed, kv_heads)
        stats = jnp.where(lane == s, high, stats)
        stats = jnp.where(lane == slots + s, total, stats)
        stats = jnp.where(lane == 2 * slots + s, owners[s].astype(f32), stats)
    packed[slots * heads :, :] = stats
    if weight_copy is not None:
        weight_copy.wait()


def project(x, weight, same, other, chunk, own=None):
    rows = x.shape[0] // 2
    for c in range(0, same.shape[1], chunk):
        product = jnp.dot(x, weight[:, c : c + chunk], preferred_element_type=f32)
        same[:, c : c + chunk] = product[:rows].astype(same.dtype)
        other[:, c : c + chunk] = product[rows:].astype(other.dtype)
        if own is not None:
            own[:, c : c + chunk] = product[:rows]


def combine_kernel(*refs, groups, rows, heads, slots, ahead, last, columns, chunk):
    local = refs[:2]
    parts = refs[2 : 2 + groups]
    weight, weight_in, x_ref, free_total, same, other = refs[2 + groups : 8 + groups]
    rest = list(refs[8 + groups :])
    own = rest.pop(0) if last else None
    copy = None
    if ahead is not None:
        copy = copy_in(columns_of(weight_in, ahead, columns), rest.pop(0), rest.pop())
    mixed, high, total = rest
    flat = rows * heads
    me = lax.axis_index("group")
    first, second = me * rows, jnp.bitwise_xor(me, 1) * rows
    free = jnp.zeros((heads, LANES), f32)
    found = []
    for k in range(groups):
        stats = parts[k][slots * heads :, :]
        free = free + stats
        for s in range(slots):
            owner = stats[0, 2 * slots + s].astype(jnp.int32)
            found.append((k, s, owner))
    free_total[0] = free[0, 3 * slots].astype(jnp.int32)
    for i in range(2):
        stats = local[i][flat:, :]
        high[i * flat : (i + 1) * flat, :] = jnp.broadcast_to(stats[:, 0:1], (flat, LANES))
    slot_stats = []
    for k, s, owner in found:
        in_first = (owner >= first) & (owner < first + rows)
        in_second = (owner >= second) & (owner < second + rows)
        row = jnp.where(
            in_first, owner - first, jnp.where(in_second, owner - second + rows, 0)
        )
        mine = in_first | in_second
        at = pl.ds(pl.multiple_of(row * heads, heads), heads)
        stats = parts[k][slots * heads :, :]
        slot_high = jnp.broadcast_to(stats[:, s : s + 1], (heads, LANES))
        slot_total = jnp.broadcast_to(stats[:, slots + s : slots + s + 1], (heads, LANES))
        slot_stats.append((mine, at, slot_high, slot_total))
        high[at, :] = jnp.maximum(high[at, :], jnp.where(mine, slot_high, far_below))
    for i in range(2):
        at = slice(i * flat, (i + 1) * flat)
        stats = local[i][flat:, :]
        keep = jnp.exp(jnp.broadcast_to(stats[:, 0:1], (flat, LANES)) - high[at, :])
        mixed[at, :] = keep * local[i][:flat, :]
        total[at, :] = keep * jnp.broadcast_to(stats[:, 1:2], (flat, LANES))
    for (k, s, _), (mine, at, slot_high, slot_total) in zip(found, slot_stats):
        add = jnp.where(mine, jnp.exp(jnp.minimum(slot_high - high[at, :], 0.0)), 0.0)
        mixed[at, :] = mixed[at, :] + add * parts[k][s * heads : (s + 1) * heads, :]
        total[at, :] = total[at, :] + add * slot_total
    mixed[...] = mixed[...] / total[...]
    for h in range(heads):
        x_ref[:, h * HEAD_DIM : (h + 1) * HEAD_DIM] = mixed[
            pl.ds(h, 2 * rows, stride=heads), :
        ].astype(bf16)
    project(x_ref[...], weight, same, other, chunk, own)
    if copy is not None:
        copy.wait()


def project_kernel(x_ref, weight, weight_in, same, other, *rest, ahead, last, columns, chunk):
    rest = list(rest)
    own = rest.pop(0) if last else None
    copy = None
    if ahead is not None:
        copy = copy_in(columns_of(weight_in, ahead, columns), *rest)
    project(x_ref[...], weight, same, other, chunk, own)
    if copy is not None:
        copy.wait()


def sum_kernel(own, final, *refs):
    total = jnp.where(lax.axis_index("group") % 2 == 0, own[...], final[...].astype(f32))
    for part in refs[:-1]:
        total = total + part[...].astype(f32)
    refs[-1][...] = total.astype(bf16)


def send_block(value, step, cross):
    groups, tp = lax.axis_size("group"), lax.axis_size("tp")
    pairs = [
        (g * tp + z, (g ^ cross) * tp + (z ^ step_mask(g, step)))
        for g in range(groups)
        for z in range(tp)
        if cross or step_mask(g, step)
    ]
    return lax.ppermute(value, ("group", "tp"), pairs)


def swap(value, axis, mask):
    size = lax.axis_size(axis)
    return lax.ppermute(value, axis, [(i, i ^ mask) for i in range(size)])


def gather_group(value):
    groups = lax.axis_size("group")
    found = [None] * groups
    found[0] = value
    found[1] = swap(value, "group", 1)
    for k in range(2, groups, 2):
        found[k] = swap(value, "group", k)
    for k in range(2, groups, 2):
        found[k + 1] = swap(found[k], "group", 1)
    return found


def step(
    queries,
    cache_keys,
    cache_values,
    pool_keys,
    pool_values,
    row_lengths,
    slot_owner,
    slot_fill,
    free_counts,
    out_weight,
):
    groups, tp = lax.axis_size("group"), lax.axis_size("tp")
    rows, width = queries.shape
    heads = width // HEAD_DIM
    kv_heads = cache_keys.shape[2] // HEAD_DIM
    slots, positions = pool_keys.shape[:2]
    columns = out_weight.shape[1] // tp
    chunk = math.gcd(columns, 512)
    sizes = dict(rows=rows, heads=heads)

    shards = gather_group(queries)
    queries, row_lengths, slot_owner, slot_fill, out_weight = (
        pltpu.with_memory_space_constraint(argument, pltpu.MemorySpace.HBM)
        for argument in (queries, row_lengths, slot_owner, slot_fill, out_weight)
    )
    copies = pltpu.SemaphoreType.DMA

    order = list(range(tp // 2 - 1, -1, -1))
    held = jax.ShapeDtypeStruct((width, columns), out_weight.dtype)
    moved = 2 * width * columns
    weights = {}

    token = call(open_kernel, jax.ShapeDtypeStruct((8, LANES), f32), [HBM], vmem=1 << 20)(
        out_weight
    )
    local, own_queries, weights[order[0]] = call(
        lambda *refs: local_kernel(
            *refs, kv_heads=kv_heads, step=order[0], columns=columns, **sizes
        ),
        [
            jax.ShapeDtypeStruct((2 * rows * heads, LANES), f32),
            jax.ShapeDtypeStruct(queries.shape, queries.dtype),
            held,
        ],
        [HBM, HBM, VMEM, VMEM, HBM, VMEM],
        scratch=[
            pltpu.SMEM(row_lengths.shape, jnp.int32),
            pltpu.VMEM((rows * heads, HEAD_DIM), f32),
            pltpu.VMEM((rows * heads, cache_keys.shape[1]), f32),
            pltpu.VMEM((rows, heads, cache_keys.shape[1]), bf16),
            copies((3,)),
        ],
        moved=moved,
        vmem=4 << 20,
    )(row_lengths, queries, cache_keys, cache_values, out_weight, token)
    shards[0] = own_queries
    pair_local = swap(local, "group", 1)

    ahead = order[1] if len(order) > 1 else None
    packed, *more = call(
        lambda *refs: slot_kernel(
            *refs,
            groups=groups,
            kv_heads=kv_heads,
            slots=slots,
            chunk=math.gcd(positions, 512),
            ahead=ahead,
            columns=columns,
            **sizes,
        ),
        [jax.ShapeDtypeStruct(((slots + 1) * heads, LANES), f32)] + [held] * (ahead is not None),
        [HBM] * 2 + [SMEM] + [VMEM] * (groups + 2) + [HBM],
        scratch=[
            pltpu.SMEM(slot_owner.shape, jnp.int32),
            pltpu.SMEM(slot_fill.shape, jnp.int32),
            pltpu.VMEM((slots * heads, HEAD_DIM), f32),
            pltpu.VMEM((slots * heads, positions), f32),
            copies((3,)),
        ],
        moved=moved,
        vmem=4 << 20,
    )(slot_owner, slot_fill, free_counts, *shards, pool_keys, pool_values, out_weight)
    if more:
        weights[ahead] = more[0]

    far = gather_group(packed)

    block = jax.ShapeDtypeStruct((rows, columns), bf16)
    whole = jax.ShapeDtypeStruct((rows, columns), f32)
    received = []
    for i, step in enumerate(order):
        last = step == 0
        ahead = order[i + 2] if i + 2 < len(order) else None
        outs = [block] * 2 + [whole] * last + [held] * (ahead is not None)
        settings = dict(ahead=ahead, last=last, columns=columns, chunk=chunk)
        if i == 0:
            x, free_total, same, other, *more = call(
                lambda *refs: combine_kernel(
                    *refs, groups=groups, slots=slots, **settings, **sizes
                ),
                [
                    jax.ShapeDtypeStruct((2 * rows, width), bf16),
                    jax.ShapeDtypeStruct((1,), jnp.int32),
                ]
                + outs,
                [VMEM] * (2 + groups + 1) + [HBM],
                out_specs=[VMEM, SMEM] + [VMEM] * len(outs),
                scratch=[pltpu.VMEM((2 * rows * heads, LANES), f32)] * 3
                + [copies] * (ahead is not None),
                moved=moved,
            )(local, pair_local, *far, weights[step], out_weight)
        else:
            same, other, *more = call(
                lambda *refs, settings=settings: project_kernel(*refs, **settings),
                outs,
                [VMEM] * 2 + [HBM],
                scratch=[copies] * (ahead is not None),
                moved=moved,
                vmem=4 << 20,
            )(x, weights[step], out_weight)
        if last:
            own = more.pop(0)
        if ahead is not None:
            weights[ahead] = more.pop(0)
        received.append(send_block(same, step, 0))
        received.append(send_block(other, step, 1))
    final = received.pop(-2)
    mixed_out = call(sum_kernel, block, [VMEM] * (2 + len(received)))(
        own, final, *received
    )
    return (mixed_out, free_total)


def solution(mesh):
    in_specs = (
        P("group", "tp"),
        P("group", None, "tp"),
        P("group", None, "tp"),
        P("group", None, "tp"),
        P("group", None, "tp"),
        P("group"),
        P("group"),
        P("group"),
        P("group"),
        P("tp", None),
    )
    out_specs = (P("group", "tp"), P())
    return jax.shard_map(step, mesh=mesh, in_specs=in_specs, out_specs=out_specs, check_vma=False)
```

```python
import math

import jax
import jax.numpy as jnp
from jax import lax
from jax.experimental import pallas as pl
from jax.experimental.pallas import tpu as pltpu
from jax.sharding import PartitionSpec as P


HEAD_DIM = 128
LANES = 128
far_below = -1e30


VMEM = pl.BlockSpec(memory_space=pltpu.VMEM)
SMEM = pl.BlockSpec(memory_space=pltpu.SMEM)
HBM = pl.BlockSpec(memory_space=pltpu.MemorySpace.HBM)
f32 = jnp.float32
bf16 = jnp.bfloat16


def call(kernel, outs, ins, scratch=(), out_specs=None, flops=0, moved=0, vmem=8 << 20):
    return pl.pallas_call(
        kernel,
        out_shape=outs,
        in_specs=ins,
        out_specs=out_specs if out_specs is not None else jax.tree.map(lambda _: VMEM, outs),
        scratch_shapes=scratch,
        cost_estimate=pl.CostEstimate(flops=flops, bytes_accessed=moved, transcendentals=0),
        compiler_params=pltpu.CompilerParams(vmem_limit_bytes=vmem),
    )


def spread_heads(tile, kv_heads):
    if kv_heads == 1:
        return tile
    heads = tile.shape[0]
    owner = lax.broadcasted_iota(jnp.int32, tile.shape, 0) // (heads // kv_heads)
    return jnp.concatenate(
        [jnp.where(owner == k, tile, jnp.zeros_like(tile)) for k in range(kv_heads)], axis=1
    )


def own_columns(wide, kv_heads):
    if kv_heads == 1:
        return wide
    heads = wide.shape[0]
    owner = lax.broadcasted_iota(jnp.int32, (heads, HEAD_DIM), 0) // (heads // kv_heads)
    picked = wide[:, :HEAD_DIM]
    for k in range(1, kv_heads):
        picked = jnp.where(owner == k, wide[:, k * HEAD_DIM : (k + 1) * HEAD_DIM], picked)
    return picked


def scores_of(query, keys):
    return lax.dot_general(
        query, keys, (((1,), (1,)), ((), ())), preferred_element_type=f32
    ) * (1.0 / math.sqrt(HEAD_DIM))


def copy_in(source, target, sem):
    copy = pltpu.make_async_copy(source, target, sem)
    copy.start()
    return copy


def open_kernel(_, token):
    token[...] = jnp.zeros_like(token)


def local_kernel(
    lengths_in, q_in, keys, values, _, __,
    packed, q_ref,
    lengths, q_heads, scores, weights, sems,
    *, rows, heads, kv_heads,
):
    positions = keys.shape[1]
    lengths_copy = copy_in(lengths_in, lengths, sems.at[0])
    q_copy = copy_in(q_in, q_ref, sems.at[1])
    q_copy.wait()
    wide = q_ref[...].astype(f32)
    for h in range(heads):
        q_heads[pl.ds(h, rows, stride=heads), :] = wide[:, h * HEAD_DIM : (h + 1) * HEAD_DIM]
    lengths_copy.wait()
    place = lax.broadcasted_iota(jnp.int32, (heads, positions), 1)
    lane = lax.broadcasted_iota(jnp.int32, (heads, LANES), 1)
    for r in range(rows):
        at = pl.ds(r * heads, heads)
        query = spread_heads(q_heads[at, :].astype(bf16), kv_heads)
        scores[at, :] = jnp.where(place < lengths[r], scores_of(query, keys[r]), far_below)
    for r in range(rows):
        at = pl.ds(r * heads, heads)
        masked = scores[at, :]
        high = jnp.max(masked, axis=-1, keepdims=True)
        weight_of = jnp.where(place < lengths[r], jnp.exp(masked - high), 0.0)
        total = jnp.sum(weight_of, axis=-1, keepdims=True)
        weights[r] = weight_of.astype(bf16)
        packed[pl.ds((rows + r) * heads, heads), :] = jnp.where(lane == 0, high, total)
    for r in range(rows):
        mixed = jnp.dot(weights[r], values[r], preferred_element_type=f32)
        packed[pl.ds(r * heads, heads), :] = own_columns(mixed, kv_heads)


def step_mask(group, step):
    return 2 * step + group % 2


def piece_of(weight, piece, columns):
    step, half = piece
    place = jnp.bitwise_xor(lax.axis_index("tp"), step_mask(lax.axis_index("group"), step))
    depth = weight.shape[0] // 2
    return weight.at[
        pl.ds(half * depth, depth), pl.ds(pl.multiple_of(place * columns, columns), columns)
    ]


def fetch(weight, pieces, targets, sems, columns):
    return [
        copy_in(piece_of(weight, piece, columns), target, sems.at[i])
        for i, (piece, target) in enumerate(zip(pieces, targets))
    ]


def fetch_kernel(weight, _, *rest, pieces, columns):
    for copy in fetch(weight, pieces, rest[:-1], rest[-1], columns):
        copy.wait()


def slot_kernel(*refs, groups, rows, heads, kv_heads, slots, chunk, pieces, columns):
    owners_in, fills_in, free = refs[:3]
    shards = refs[3 : 3 + groups]
    keys, values, weight_in = refs[3 + groups : 6 + groups]
    packed, *rest = refs[6 + groups :]
    owners, fills, q_heads, scores, sems, fetch_sems = rest[len(pieces) :]
    weight_copies = fetch(weight_in, pieces, rest, fetch_sems, columns)
    copies = [
        copy_in(owners_in, owners, sems.at[0]),
        copy_in(fills_in, fills, sems.at[1]),
    ]
    for copy in copies:
        copy.wait()
    positions = keys.shape[1]
    me = lax.axis_index("group")
    row_at = lax.broadcasted_iota(jnp.int32, (rows, heads * HEAD_DIM), 0)
    for s in range(slots):
        owner = jnp.maximum(owners[s], 0)
        home = lax.div(owner, rows)
        row = lax.rem(owner, rows)
        for k in range(groups):

            @pl.when(jnp.bitwise_xor(home, me) == k)
            def _(k=k, s=s, row=row):
                block = jnp.where(row_at == row, shards[k][...].astype(f32), 0.0)
                single = jnp.sum(block, axis=0, keepdims=True)
                for h in range(heads):
                    q_heads[s * heads + h : s * heads + h + 1, :] = single[
                        :, h * HEAD_DIM : (h + 1) * HEAD_DIM
                    ]

    place = lax.broadcasted_iota(jnp.int32, (heads, positions), 1)
    lane = lax.broadcasted_iota(jnp.int32, (heads, LANES), 1)
    stats = jnp.where(lane == 3 * slots, free[0].astype(f32), 0.0)
    for s in range(slots):
        at = pl.ds(s * heads, heads)
        query = spread_heads(q_heads[at, :].astype(bf16), kv_heads)
        for c in range(0, positions, chunk):
            scores[at, c : c + chunk] = scores_of(query, keys[s, c : c + chunk, :])
    for s in range(slots):
        at = pl.ds(s * heads, heads)
        visible = place < fills[s]
        masked = jnp.where(visible, scores[at, :], far_below)
        high = jnp.max(masked, axis=-1, keepdims=True)
        weights = jnp.where(visible, jnp.exp(masked - high), 0.0)
        total = jnp.sum(weights, axis=-1, keepdims=True)
        mixed = jnp.dot(weights.astype(bf16), values[s], preferred_element_type=f32)
        packed[at, :] = own_columns(mixed, kv_heads)
        stats = jnp.where(lane == s, high, stats)
        stats = jnp.where(lane == slots + s, total, stats)
        stats = jnp.where(lane == 2 * slots + s, owners[s].astype(f32), stats)
    packed[slots * heads :, :] = stats
    for copy in weight_copies:
        copy.wait()


def project(x, halves, same, other, chunk, own=None):
    rows, depth = x.shape[0] // 2, x.shape[1] // 2
    for c in range(0, same.shape[1], chunk):
        at = slice(c, c + chunk)
        product = jnp.dot(
            x[:, :depth], halves[0][:, at], preferred_element_type=f32
        ) + jnp.dot(x[:, depth:], halves[1][:, at], preferred_element_type=f32)
        same[:, at] = product[:rows].astype(same.dtype)
        other[:, at] = product[rows:].astype(other.dtype)
        if own is not None:
            own[:, at] = product[:rows]


def combine_kernel(*refs, rows, heads, slots, pieces, last, columns, chunk):
    local, gathered, halves = refs[:2], refs[2:4], refs[4:6]
    weight_in, x_ref, free_total, same, other, *rest = refs[6:]
    own = rest.pop(0) if last else None
    mixed, high, total, sems = rest[len(pieces) :]
    copies = fetch(weight_in, pieces, rest, sems, columns)
    flat, each = rows * heads, (slots + 1) * heads
    me = lax.axis_index("group")
    first, second = me * rows, jnp.bitwise_xor(me, 1) * rows
    free = jnp.zeros((heads, LANES), f32)
    found = []
    for part in gathered:
        for k in range(0, part.shape[0], each):
            stats = part[k + slots * heads : k + each, :]
            free = free + stats
            for s in range(slots):
                owner = stats[0, 2 * slots + s].astype(jnp.int32)
                found.append((part, k, s, stats, owner))
    free_total[0] = free[0, 3 * slots].astype(jnp.int32)
    for i in range(2):
        stats = local[i][flat:, :]
        high[i * flat : (i + 1) * flat, :] = jnp.broadcast_to(stats[:, 0:1], (flat, LANES))
    slot_stats = []
    for part, k, s, stats, owner in found:
        in_first = (owner >= first) & (owner < first + rows)
        in_second = (owner >= second) & (owner < second + rows)
        row = jnp.where(
            in_first, owner - first, jnp.where(in_second, owner - second + rows, 0)
        )
        mine = in_first | in_second
        at = pl.ds(pl.multiple_of(row * heads, heads), heads)
        slot_high = jnp.broadcast_to(stats[:, s : s + 1], (heads, LANES))
        slot_total = jnp.broadcast_to(stats[:, slots + s : slots + s + 1], (heads, LANES))
        slot_stats.append((part, k + s * heads, mine, at, slot_high, slot_total))
        high[at, :] = jnp.maximum(high[at, :], jnp.where(mine, slot_high, far_below))
    for i in range(2):
        at = slice(i * flat, (i + 1) * flat)
        stats = local[i][flat:, :]
        keep = jnp.exp(jnp.broadcast_to(stats[:, 0:1], (flat, LANES)) - high[at, :])
        mixed[at, :] = keep * local[i][:flat, :]
        total[at, :] = keep * jnp.broadcast_to(stats[:, 1:2], (flat, LANES))
    for part, k, mine, at, slot_high, slot_total in slot_stats:
        add = jnp.where(mine, jnp.exp(jnp.minimum(slot_high - high[at, :], 0.0)), 0.0)
        mixed[at, :] = mixed[at, :] + add * part[k : k + heads, :]
        total[at, :] = total[at, :] + add * slot_total
    mixed[...] = mixed[...] / total[...]
    for h in range(heads):
        x_ref[:, h * HEAD_DIM : (h + 1) * HEAD_DIM] = mixed[
            pl.ds(h, 2 * rows, stride=heads), :
        ].astype(bf16)
    project(x_ref[...], halves, same, other, chunk, own)
    for copy in copies:
        copy.wait()


def project_kernel(x_ref, *refs, pieces, last, columns, chunk):
    halves = refs[:2]
    weight_in, same, other, *rest = refs[2:]
    own = rest.pop(0) if last else None
    copies = fetch(weight_in, pieces, rest, rest[-1], columns)
    project(x_ref[...], halves, same, other, chunk, own)
    for copy in copies:
        copy.wait()


def sum_kernel(own, final, *refs):
    total = jnp.where(lax.axis_index("group") % 2 == 0, own[...], final[...].astype(f32))
    for part in refs[:-1]:
        total = total + part[...].astype(f32)
    refs[-1][...] = total.astype(bf16)


def send_block(value, step, cross):
    groups, tp = lax.axis_size("group"), lax.axis_size("tp")
    pairs = [
        (g * tp + z, (g ^ cross) * tp + (z ^ step_mask(g, step)))
        for g in range(groups)
        for z in range(tp)
        if cross or step_mask(g, step)
    ]
    return lax.ppermute(value, ("group", "tp"), pairs)


def swap(value, axis, mask):
    size = lax.axis_size(axis)
    return lax.ppermute(value, axis, [(i, i ^ mask) for i in range(size)])


def pair_masks(groups):
    return [1 << i for i in range(1, (groups - 1).bit_length())]


def gather_group(value):
    groups = lax.axis_size("group")
    found = [None] * groups
    found[0] = value
    found[1] = swap(value, "group", 1)
    for k in range(2, groups, 2):
        found[k] = swap(value, "group", k)
    for k in range(2, groups, 2):
        found[k + 1] = swap(found[k], "group", 1)
    return found


def step(
    queries,
    cache_keys,
    cache_values,
    pool_keys,
    pool_values,
    row_lengths,
    slot_owner,
    slot_fill,
    free_counts,
    out_weight,
):
    groups, tp = lax.axis_size("group"), lax.axis_size("tp")
    rows, width = queries.shape
    heads = width // HEAD_DIM
    kv_heads = cache_keys.shape[2] // HEAD_DIM
    slots, positions = pool_keys.shape[:2]
    columns = out_weight.shape[1] // tp
    chunk = math.gcd(columns, 512)
    sizes = dict(rows=rows, heads=heads)

    shards = gather_group(queries)
    queries, row_lengths, slot_owner, slot_fill, out_weight = (
        pltpu.with_memory_space_constraint(argument, pltpu.MemorySpace.HBM)
        for argument in (queries, row_lengths, slot_owner, slot_fill, out_weight)
    )
    copies = pltpu.SemaphoreType.DMA

    order = list(range(tp // 2 - 1, -1, -1))
    pieces = [(step, half) for step in order for half in range(2)]
    held = jax.ShapeDtypeStruct((width // 2, columns), out_weight.dtype)
    piece_bytes = width * columns
    weights = {}

    def take(count):
        taken = pieces[:count]
        del pieces[:count]
        return taken

    token = call(open_kernel, jax.ShapeDtypeStruct((8, LANES), f32), [HBM], vmem=1 << 20)(
        out_weight
    )
    local, own_queries = call(
        lambda *refs: local_kernel(*refs, kv_heads=kv_heads, **sizes),
        [
            jax.ShapeDtypeStruct((2 * rows * heads, LANES), f32),
            jax.ShapeDtypeStruct(queries.shape, queries.dtype),
        ],
        [HBM, HBM, VMEM, VMEM, HBM, VMEM],
        scratch=[
            pltpu.SMEM(row_lengths.shape, jnp.int32),
            pltpu.VMEM((rows * heads, HEAD_DIM), f32),
            pltpu.VMEM((rows * heads, cache_keys.shape[1]), f32),
            pltpu.VMEM((rows, heads, cache_keys.shape[1]), bf16),
            copies((2,)),
        ],
        moved=2 * (cache_keys.size + cache_values.size),
        vmem=4 << 20,
    )(row_lengths, queries, cache_keys, cache_values, out_weight, token)
    shards[0] = own_queries
    pair_local = swap(local, "group", 1)

    taken = take(1)
    packed, *more = call(
        lambda *refs, taken=taken: slot_kernel(
            *refs,
            groups=groups,
            kv_heads=kv_heads,
            slots=slots,
            chunk=math.gcd(positions, 512),
            pieces=taken,
            columns=columns,
            **sizes,
        ),
        [jax.ShapeDtypeStruct(((slots + 1) * heads, LANES), f32)] + [held] * len(taken),
        [HBM] * 2 + [SMEM] + [VMEM] * (groups + 2) + [HBM],
        scratch=[
            pltpu.SMEM(slot_owner.shape, jnp.int32),
            pltpu.SMEM(slot_fill.shape, jnp.int32),
            pltpu.VMEM((slots * heads, HEAD_DIM), f32),
            pltpu.VMEM((slots * heads, positions), f32),
            copies((2,)),
            copies((1,)),
        ],
        moved=2 * (pool_keys.size + pool_values.size),
        vmem=4 << 20,
    )(slot_owner, slot_fill, free_counts, *shards, pool_keys, pool_values, out_weight)
    weights.update(zip(taken, more))

    gathered = packed
    for mask in pair_masks(groups):
        other = swap(gathered, "group", mask)
        taken = take(1)
        if taken:
            more = call(
                lambda *refs, taken=taken: fetch_kernel(*refs, pieces=taken, columns=columns),
                [held] * len(taken),
                [HBM, pl.BlockSpec(memory_space=pl.ANY)],
                scratch=[copies((1,))],
                moved=piece_bytes,
                vmem=1 << 20,
            )(out_weight, packed)
            weights.update(zip(taken, more))
        gathered = jnp.concatenate([gathered, other], axis=0)
    pair_gathered = swap(gathered, "group", 1)

    block = jax.ShapeDtypeStruct((rows, columns), bf16)
    whole = jax.ShapeDtypeStruct((rows, columns), f32)
    received = []
    for i, step in enumerate(order):
        last = step == 0
        taken = take(max(0, len(pieces) - 2 * (len(order) - 2 - i)))
        outs = [block] * 2 + [whole] * last + [held] * len(taken)
        settings = dict(pieces=taken, last=last, columns=columns, chunk=chunk)
        halves = [weights[step, half] for half in range(2)]
        moved = piece_bytes * max(2, len(taken))
        if i == 0:
            x, free_total, same, other, *more = call(
                lambda *refs: combine_kernel(*refs, slots=slots, **settings, **sizes),
                [
                    jax.ShapeDtypeStruct((2 * rows, width), bf16),
                    jax.ShapeDtypeStruct((1,), jnp.int32),
                ]
                + outs,
                [VMEM] * 6 + [HBM],
                out_specs=[VMEM, SMEM] + [VMEM] * len(outs),
                scratch=[pltpu.VMEM((2 * rows * heads, LANES), f32)] * 3
                + [copies((max(1, len(taken)),))],
                moved=moved,
            )(local, pair_local, gathered, pair_gathered, *halves, out_weight)
        else:
            same, other, *more = call(
                lambda *refs, settings=settings: project_kernel(*refs, **settings),
                outs,
                [VMEM] * 3 + [HBM],
                scratch=[copies((max(1, len(taken)),))],
                moved=moved,
                vmem=4 << 20,
            )(x, *halves, out_weight)
        if last:
            own = more.pop(0)
        weights.update(zip(taken, more))
        received.append(send_block(same, step, 0))
        received.append(send_block(other, step, 1))
    final = received.pop(-2)
    mixed_out = call(sum_kernel, block, [VMEM] * (2 + len(received)))(
        own, final, *received
    )
    return (mixed_out, free_total)


def solution(mesh):
    in_specs = (
        P("group", "tp"),
        P("group", None, "tp"),
        P("group", None, "tp"),
        P("group", None, "tp"),
        P("group", None, "tp"),
        P("group"),
        P("group"),
        P("group"),
        P("group"),
        P("tp", None),
    )
    out_specs = (P("group", "tp"), P())
    return jax.shard_map(step, mesh=mesh, in_specs=in_specs, out_specs=out_specs, check_vma=False)
```

```python
import math

import jax
import jax.numpy as jnp
from jax import lax
from jax.experimental import pallas as pl
from jax.experimental.pallas import tpu as pltpu
from jax.sharding import PartitionSpec as P


HEAD_DIM = 128
LANES = 128
far_below = -1e30


VMEM = pl.BlockSpec(memory_space=pltpu.VMEM)
SMEM = pl.BlockSpec(memory_space=pltpu.SMEM)
HBM = pl.BlockSpec(memory_space=pltpu.MemorySpace.HBM)
f32 = jnp.float32
bf16 = jnp.bfloat16


def call(kernel, outs, ins, scratch=(), out_specs=None, flops=0, moved=0, vmem=8 << 20):
    return pl.pallas_call(
        kernel,
        out_shape=outs,
        in_specs=ins,
        out_specs=out_specs if out_specs is not None else jax.tree.map(lambda _: VMEM, outs),
        scratch_shapes=scratch,
        cost_estimate=pl.CostEstimate(flops=flops, bytes_accessed=moved, transcendentals=0),
        compiler_params=pltpu.CompilerParams(vmem_limit_bytes=vmem),
    )


def spread_heads(tile, kv_heads):
    if kv_heads == 1:
        return tile
    heads = tile.shape[0]
    owner = lax.broadcasted_iota(jnp.int32, tile.shape, 0) // (heads // kv_heads)
    return jnp.concatenate(
        [jnp.where(owner == k, tile, jnp.zeros_like(tile)) for k in range(kv_heads)], axis=1
    )


def own_columns(wide, kv_heads):
    if kv_heads == 1:
        return wide
    heads = wide.shape[0]
    owner = lax.broadcasted_iota(jnp.int32, (heads, HEAD_DIM), 0) // (heads // kv_heads)
    picked = wide[:, :HEAD_DIM]
    for k in range(1, kv_heads):
        picked = jnp.where(owner == k, wide[:, k * HEAD_DIM : (k + 1) * HEAD_DIM], picked)
    return picked


def scores_of(query, keys):
    return lax.dot_general(
        query, keys, (((1,), (1,)), ((), ())), preferred_element_type=f32
    ) * (1.0 / math.sqrt(HEAD_DIM))


def copy_in(source, target, sem):
    copy = pltpu.make_async_copy(source, target, sem)
    copy.start()
    return copy


def open_kernel(_, token):
    token[...] = jnp.zeros_like(token)


def local_kernel(
    lengths_in, q_in, keys, values, weight_in, _, packed, q_ref, *rest,
    rows, heads, kv_heads, pieces, columns,
):
    lengths, q_heads, scores, weights, sems, fetch_sems = rest[len(pieces) :]
    positions = keys.shape[1]
    lengths_copy = copy_in(lengths_in, lengths, sems.at[0])
    q_copy = copy_in(q_in, q_ref, sems.at[1])
    weight_copies = fetch(weight_in, pieces, rest, fetch_sems, columns)
    q_copy.wait()
    wide = q_ref[...].astype(f32)
    for h in range(heads):
        q_heads[pl.ds(h, rows, stride=heads), :] = wide[:, h * HEAD_DIM : (h + 1) * HEAD_DIM]
    lengths_copy.wait()
    place = lax.broadcasted_iota(jnp.int32, (heads, positions), 1)
    lane = lax.broadcasted_iota(jnp.int32, (heads, LANES), 1)
    for r in range(rows):
        at = pl.ds(r * heads, heads)
        query = spread_heads(q_heads[at, :].astype(bf16), kv_heads)
        scores[at, :] = jnp.where(place < lengths[r], scores_of(query, keys[r]), far_below)
    for r in range(rows):
        at = pl.ds(r * heads, heads)
        masked = scores[at, :]
        high = jnp.max(masked, axis=-1, keepdims=True)
        weight_of = jnp.where(place < lengths[r], jnp.exp(masked - high), 0.0)
        total = jnp.sum(weight_of, axis=-1, keepdims=True)
        weights[r] = weight_of.astype(bf16)
        packed[pl.ds((rows + r) * heads, heads), :] = jnp.where(lane == 0, high, total)
    for r in range(rows):
        mixed = jnp.dot(weights[r], values[r], preferred_element_type=f32)
        packed[pl.ds(r * heads, heads), :] = own_columns(mixed, kv_heads)
    for copy in weight_copies:
        copy.wait()


def step_mask(group, step):
    return 2 * step + group % 2


def piece_of(weight, piece, columns):
    step, half = piece
    place = jnp.bitwise_xor(lax.axis_index("tp"), step_mask(lax.axis_index("group"), step))
    depth = weight.shape[0] // 2
    return weight.at[
        pl.ds(half * depth, depth), pl.ds(pl.multiple_of(place * columns, columns), columns)
    ]


def fetch(weight, pieces, targets, sems, columns):
    copies = [
        pltpu.make_async_copy(piece_of(weight, piece, columns), target, sems.at[i])
        for i, (piece, target) in enumerate(zip(pieces, targets))
    ]

    @pl.when(lax.axis_index("group") >= 0)
    def _():
        for copy in copies:
            copy.start()

    return copies


def fetch_kernel(weight, _, *rest, pieces, columns):
    for copy in fetch(weight, pieces, rest[:-1], rest[-1], columns):
        copy.wait()


def slot_kernel(*refs, groups, rows, heads, kv_heads, slots, chunk, pieces, columns):
    owners_in, fills_in, free = refs[:3]
    shards = refs[3 : 3 + groups]
    keys, values, weight_in = refs[3 + groups : 6 + groups]
    packed, *rest = refs[6 + groups :]
    owners, fills, q_heads, scores, sems, fetch_sems = rest[len(pieces) :]
    weight_copies = fetch(weight_in, pieces, rest, fetch_sems, columns)
    copies = [
        copy_in(owners_in, owners, sems.at[0]),
        copy_in(fills_in, fills, sems.at[1]),
    ]
    for copy in copies:
        copy.wait()
    positions = keys.shape[1]
    me = lax.axis_index("group")
    row_at = lax.broadcasted_iota(jnp.int32, (rows, heads * HEAD_DIM), 0)
    for s in range(slots):
        owner = jnp.maximum(owners[s], 0)
        home = lax.div(owner, rows)
        row = lax.rem(owner, rows)
        for k in range(groups):

            @pl.when(jnp.bitwise_xor(home, me) == k)
            def _(k=k, s=s, row=row):
                block = jnp.where(row_at == row, shards[k][...].astype(f32), 0.0)
                single = jnp.sum(block, axis=0, keepdims=True)
                for h in range(heads):
                    q_heads[s * heads + h : s * heads + h + 1, :] = single[
                        :, h * HEAD_DIM : (h + 1) * HEAD_DIM
                    ]

    place = lax.broadcasted_iota(jnp.int32, (heads, positions), 1)
    lane = lax.broadcasted_iota(jnp.int32, (heads, LANES), 1)
    stats = jnp.where(lane == 3 * slots, free[0].astype(f32), 0.0)
    for s in range(slots):
        at = pl.ds(s * heads, heads)
        query = spread_heads(q_heads[at, :].astype(bf16), kv_heads)
        for c in range(0, positions, chunk):
            scores[at, c : c + chunk] = scores_of(query, keys[s, c : c + chunk, :])
    for s in range(slots):
        at = pl.ds(s * heads, heads)
        visible = place < fills[s]
        masked = jnp.where(visible, scores[at, :], far_below)
        high = jnp.max(masked, axis=-1, keepdims=True)
        weights = jnp.where(visible, jnp.exp(masked - high), 0.0)
        total = jnp.sum(weights, axis=-1, keepdims=True)
        mixed = jnp.dot(weights.astype(bf16), values[s], preferred_element_type=f32)
        packed[at, :] = own_columns(mixed, kv_heads)
        stats = jnp.where(lane == s, high, stats)
        stats = jnp.where(lane == slots + s, total, stats)
        stats = jnp.where(lane == 2 * slots + s, owners[s].astype(f32), stats)
    packed[slots * heads :, :] = stats
    for copy in weight_copies:
        copy.wait()


def project(x, halves, same, other, chunk, own=None):
    rows, depth = x.shape[0] // 2, x.shape[1] // 2
    for c in range(0, same.shape[1], chunk):
        at = slice(c, c + chunk)
        product = jnp.dot(
            x[:, :depth], halves[0][:, at], preferred_element_type=f32
        ) + jnp.dot(x[:, depth:], halves[1][:, at], preferred_element_type=f32)
        same[:, at] = product[:rows].astype(same.dtype)
        other[:, at] = product[rows:].astype(other.dtype)
        if own is not None:
            own[:, at] = product[:rows]


def combine_kernel(*refs, groups, rows, heads, slots, pieces, last, columns, chunk):
    local, gathered, halves = refs[:2], refs[2 : 2 + groups], refs[2 + groups : 4 + groups]
    weight_in, x_ref, free_total, same, other, *rest = refs[4 + groups :]
    own = rest.pop(0) if last else None
    mixed, high, total, sems = rest[len(pieces) :]
    copies = fetch(weight_in, pieces, rest, sems, columns)
    flat, each = rows * heads, (slots + 1) * heads
    me = lax.axis_index("group")
    first, second = me * rows, jnp.bitwise_xor(me, 1) * rows
    free = jnp.zeros((heads, LANES), f32)
    found = []
    for part in gathered:
        for k in range(0, part.shape[0], each):
            stats = part[k + slots * heads : k + each, :]
            free = free + stats
            for s in range(slots):
                owner = stats[0, 2 * slots + s].astype(jnp.int32)
                found.append((part, k, s, stats, owner))
    free_total[0] = free[0, 3 * slots].astype(jnp.int32)
    for i in range(2):
        stats = local[i][flat:, :]
        high[i * flat : (i + 1) * flat, :] = jnp.broadcast_to(stats[:, 0:1], (flat, LANES))
    slot_stats = []
    for part, k, s, stats, owner in found:
        in_first = (owner >= first) & (owner < first + rows)
        in_second = (owner >= second) & (owner < second + rows)
        row = jnp.where(
            in_first, owner - first, jnp.where(in_second, owner - second + rows, 0)
        )
        mine = in_first | in_second
        at = pl.ds(pl.multiple_of(row * heads, heads), heads)
        slot_high = jnp.broadcast_to(stats[:, s : s + 1], (heads, LANES))
        slot_total = jnp.broadcast_to(stats[:, slots + s : slots + s + 1], (heads, LANES))
        slot_stats.append((part, k + s * heads, mine, at, slot_high, slot_total))
        high[at, :] = jnp.maximum(high[at, :], jnp.where(mine, slot_high, far_below))
    for i in range(2):
        at = slice(i * flat, (i + 1) * flat)
        stats = local[i][flat:, :]
        keep = jnp.exp(jnp.broadcast_to(stats[:, 0:1], (flat, LANES)) - high[at, :])
        mixed[at, :] = keep * local[i][:flat, :]
        total[at, :] = keep * jnp.broadcast_to(stats[:, 1:2], (flat, LANES))
    for part, k, mine, at, slot_high, slot_total in slot_stats:
        add = jnp.where(mine, jnp.exp(jnp.minimum(slot_high - high[at, :], 0.0)), 0.0)
        mixed[at, :] = mixed[at, :] + add * part[k : k + heads, :]
        total[at, :] = total[at, :] + add * slot_total
    mixed[...] = mixed[...] / total[...]
    for h in range(heads):
        x_ref[:, h * HEAD_DIM : (h + 1) * HEAD_DIM] = mixed[
            pl.ds(h, 2 * rows, stride=heads), :
        ].astype(bf16)
    project(x_ref[...], halves, same, other, chunk, own)
    for copy in copies:
        copy.wait()


def project_kernel(x_ref, *refs, pieces, last, columns, chunk):
    halves = refs[:2]
    weight_in, same, other, *rest = refs[2:]
    own = rest.pop(0) if last else None
    copies = fetch(weight_in, pieces, rest, rest[-1], columns)
    project(x_ref[...], halves, same, other, chunk, own)
    for copy in copies:
        copy.wait()


def pick_kernel(even, odd, out):
    first = lax.axis_index("group") % 2 == 0

    @pl.when(first)
    def _():
        out[...] = even[...]

    @pl.when(jnp.logical_not(first))
    def _():
        out[...] = odd[...]


def sum_kernel(own, crossed, *refs):
    total = jnp.where(lax.axis_index("group") % 2 == 0, own[...], crossed[...].astype(f32))
    for part in refs[:-1]:
        total = total + part[...].astype(f32)
    refs[-1][...] = total.astype(bf16)


def send_block(value, step, crossed):
    groups, tp = lax.axis_size("group"), lax.axis_size("tp")
    pairs = [
        (g * tp + z, g * tp + (z ^ step_mask(g ^ crossed, step)))
        for g in range(groups)
        for z in range(tp)
    ]
    return lax.ppermute(value, ("group", "tp"), pairs)


def swap(value, axis, mask):
    size = lax.axis_size(axis)
    return lax.ppermute(value, axis, [(i, i ^ mask) for i in range(size)])


def gather_group(value):
    groups = lax.axis_size("group")
    found = [None] * groups
    found[0] = value
    found[1] = swap(value, "group", 1)
    for k in range(2, groups, 2):
        found[k] = swap(value, "group", k)
    for k in range(2, groups, 2):
        found[k + 1] = swap(found[k], "group", 1)
    return found


def step(
    queries,
    cache_keys,
    cache_values,
    pool_keys,
    pool_values,
    row_lengths,
    slot_owner,
    slot_fill,
    free_counts,
    out_weight,
):
    groups, tp = lax.axis_size("group"), lax.axis_size("tp")
    rows, width = queries.shape
    heads = width // HEAD_DIM
    kv_heads = cache_keys.shape[2] // HEAD_DIM
    slots, positions = pool_keys.shape[:2]
    columns = out_weight.shape[1] // tp
    chunk = math.gcd(columns, 512)
    sizes = dict(rows=rows, heads=heads)

    shards = gather_group(queries)
    queries, row_lengths, slot_owner, slot_fill, out_weight = (
        pltpu.with_memory_space_constraint(argument, pltpu.MemorySpace.HBM)
        for argument in (queries, row_lengths, slot_owner, slot_fill, out_weight)
    )
    copies = pltpu.SemaphoreType.DMA

    order = list(range(tp // 2 - 1, -1, -1))
    pieces = [(step, half) for step in order for half in range(2)]
    held = jax.ShapeDtypeStruct((width // 2, columns), out_weight.dtype)
    piece_bytes = width * columns
    weights = {}

    def take(count):
        taken = pieces[:count]
        del pieces[:count]
        return taken

    token = call(open_kernel, jax.ShapeDtypeStruct((8, LANES), f32), [HBM], vmem=1 << 20)(
        out_weight
    )
    taken = take(1)
    local, own_queries, *more = call(
        lambda *refs, taken=taken: local_kernel(
            *refs, kv_heads=kv_heads, pieces=taken, columns=columns, **sizes
        ),
        [
            jax.ShapeDtypeStruct((2 * rows * heads, LANES), f32),
            jax.ShapeDtypeStruct(queries.shape, queries.dtype),
        ]
        + [held] * len(taken),
        [HBM, HBM, VMEM, VMEM, HBM, VMEM],
        scratch=[
            pltpu.SMEM(row_lengths.shape, jnp.int32),
            pltpu.VMEM((rows * heads, HEAD_DIM), f32),
            pltpu.VMEM((rows * heads, cache_keys.shape[1]), f32),
            pltpu.VMEM((rows, heads, cache_keys.shape[1]), bf16),
            copies((2,)),
            copies((1,)),
        ],
        moved=2 * (cache_keys.size + cache_values.size),
        vmem=4 << 20,
    )(row_lengths, queries, cache_keys, cache_values, out_weight, token)
    weights.update(zip(taken, more))
    shards[0] = own_queries
    pair_local = swap(local, "group", 1)

    taken = take(1)
    packed, *more = call(
        lambda *refs, taken=taken: slot_kernel(
            *refs,
            groups=groups,
            kv_heads=kv_heads,
            slots=slots,
            chunk=math.gcd(positions, 512),
            pieces=taken,
            columns=columns,
            **sizes,
        ),
        [jax.ShapeDtypeStruct(((slots + 1) * heads, LANES), f32)] + [held] * len(taken),
        [HBM] * 2 + [SMEM] + [VMEM] * (groups + 2) + [HBM],
        scratch=[
            pltpu.SMEM(slot_owner.shape, jnp.int32),
            pltpu.SMEM(slot_fill.shape, jnp.int32),
            pltpu.VMEM((slots * heads, HEAD_DIM), f32),
            pltpu.VMEM((slots * heads, positions), f32),
            copies((2,)),
            copies((1,)),
        ],
        moved=2 * (pool_keys.size + pool_values.size),
        vmem=4 << 20,
    )(slot_owner, slot_fill, free_counts, *shards, pool_keys, pool_values, out_weight)
    weights.update(zip(taken, more))

    far = gather_group(packed)
    taken = take(1)
    more = call(
        lambda *refs, taken=taken: fetch_kernel(*refs, pieces=taken, columns=columns),
        [held] * len(taken),
        [HBM, pl.BlockSpec(memory_space=pl.ANY)],
        scratch=[copies((1,))],
        moved=piece_bytes,
        vmem=1 << 20,
    )(out_weight, packed)
    weights.update(zip(taken, more))

    block = jax.ShapeDtypeStruct((rows, columns), bf16)
    whole = jax.ShapeDtypeStruct((rows, columns), f32)
    received = []
    for i, step in enumerate(order):
        last = step == 0
        taken = take(max(0, len(pieces) - 2 * (len(order) - 2 - i)))
        outs = [block] * 2 + [whole] * last + [held] * len(taken)
        settings = dict(pieces=taken, last=last, columns=columns, chunk=chunk)
        halves = [weights[step, half] for half in range(2)]
        moved = piece_bytes * max(2, len(taken))
        if i == 0:
            x, free_total, same, other, *more = call(
                lambda *refs: combine_kernel(
                    *refs, groups=groups, slots=slots, **settings, **sizes
                ),
                [
                    jax.ShapeDtypeStruct((2 * rows, width), bf16),
                    jax.ShapeDtypeStruct((1,), jnp.int32),
                ]
                + outs,
                [VMEM] * (4 + groups) + [HBM],
                out_specs=[VMEM, SMEM] + [VMEM] * len(outs),
                scratch=[pltpu.VMEM((2 * rows * heads, LANES), f32)] * 3
                + [copies((max(1, len(taken)),))],
                moved=moved,
            )(local, pair_local, *far, *halves, out_weight)
        else:
            same, other, *more = call(
                lambda *refs, settings=settings: project_kernel(*refs, **settings),
                outs,
                [VMEM] * 3 + [HBM],
                scratch=[copies((max(1, len(taken)),))],
                moved=moved,
                vmem=4 << 20,
            )(x, *halves, out_weight)
        if last:
            own = more.pop(0)
        weights.update(zip(taken, more))
        crossed = swap(other, "group", 1)
        if last:
            leaving = call(pick_kernel, block, [VMEM] * 2, vmem=1 << 20)(crossed, same)
            received.append(swap(leaving, "tp", 1))
        else:
            received.append(send_block(same, step, 0))
            received.append(send_block(crossed, step, 1))
    mixed_out = call(sum_kernel, block, [VMEM] * (2 + len(received)))(own, crossed, *received)
    return (mixed_out, free_total)


def solution(mesh):
    in_specs = (
        P("group", "tp"),
        P("group", None, "tp"),
        P("group", None, "tp"),
        P("group", None, "tp"),
        P("group", None, "tp"),
        P("group"),
        P("group"),
        P("group"),
        P("group"),
        P("tp", None),
    )
    out_specs = (P("group", "tp"), P())
    return jax.shard_map(step, mesh=mesh, in_specs=in_specs, out_specs=out_specs, check_vma=False)
```

```python
import math

import jax
import jax.numpy as jnp
from jax import lax
from jax.experimental import pallas as pl
from jax.experimental.pallas import tpu as pltpu
from jax.sharding import PartitionSpec as P


HEAD_DIM = 128
LANES = 128
far_below = -1e30


VMEM = pl.BlockSpec(memory_space=pltpu.VMEM)
SMEM = pl.BlockSpec(memory_space=pltpu.SMEM)
HBM = pl.BlockSpec(memory_space=pltpu.MemorySpace.HBM)
f32 = jnp.float32
bf16 = jnp.bfloat16


def call(kernel, outs, ins, scratch=(), out_specs=None, flops=0, moved=0, vmem=8 << 20):
    return pl.pallas_call(
        kernel,
        out_shape=outs,
        in_specs=ins,
        out_specs=out_specs if out_specs is not None else jax.tree.map(lambda _: VMEM, outs),
        scratch_shapes=scratch,
        cost_estimate=pl.CostEstimate(flops=flops, bytes_accessed=moved, transcendentals=0),
        compiler_params=pltpu.CompilerParams(vmem_limit_bytes=vmem),
    )


def spread_heads(tile, kv_heads):
    if kv_heads == 1:
        return tile
    heads = tile.shape[0]
    owner = lax.broadcasted_iota(jnp.int32, tile.shape, 0) // (heads // kv_heads)
    return jnp.concatenate(
        [jnp.where(owner == k, tile, jnp.zeros_like(tile)) for k in range(kv_heads)], axis=1
    )


def own_columns(wide, kv_heads):
    if kv_heads == 1:
        return wide
    heads = wide.shape[0]
    owner = lax.broadcasted_iota(jnp.int32, (heads, HEAD_DIM), 0) // (heads // kv_heads)
    picked = wide[:, :HEAD_DIM]
    for k in range(1, kv_heads):
        picked = jnp.where(owner == k, wide[:, k * HEAD_DIM : (k + 1) * HEAD_DIM], picked)
    return picked


def scores_of(query, keys):
    return lax.dot_general(
        query, keys, (((1,), (1,)), ((), ())), preferred_element_type=f32
    ) * (1.0 / math.sqrt(HEAD_DIM))


def open_kernel(_, token):
    token[...] = jnp.zeros_like(token)


def local_kernel(
    lengths, q_ref, keys, values, weight_in, _, packed, *rest,
    rows, heads, kv_heads, pieces, columns,
):
    q_heads, scores, weights, fetch_sems = rest[len(pieces) :]
    positions = keys.shape[1]
    weight_copies = fetch(weight_in, pieces, rest, fetch_sems, columns)

    @region
    def _():
        wide = q_ref[...].astype(f32)
        for h in range(heads):
            q_heads[pl.ds(h, rows, stride=heads), :] = wide[:, h * HEAD_DIM : (h + 1) * HEAD_DIM]

    place = lax.broadcasted_iota(jnp.int32, (heads, positions), 1)
    lane = lax.broadcasted_iota(jnp.int32, (heads, LANES), 1)
    for r in range(rows):
        at = pl.ds(r * heads, heads)
        query = spread_heads(q_heads[at, :].astype(bf16), kv_heads)
        scores[at, :] = jnp.where(place < lengths[r], scores_of(query, keys[r]), far_below)
    for r in range(rows):
        at = pl.ds(r * heads, heads)
        masked = scores[at, :]
        high = jnp.max(masked, axis=-1, keepdims=True)
        weight_of = jnp.where(place < lengths[r], jnp.exp(masked - high), 0.0)
        total = jnp.sum(weight_of, axis=-1, keepdims=True)
        weights[r] = weight_of.astype(bf16)
        packed[pl.ds((rows + r) * heads, heads), :] = jnp.where(lane == 0, high, total)

    @region
    def _():
        for r in range(rows):
            mixed = jnp.dot(weights[r], values[r], preferred_element_type=f32)
            packed[pl.ds(r * heads, heads), :] = own_columns(mixed, kv_heads)

    for copy in weight_copies:
        copy.wait()


def step_mask(group, step):
    return 2 * step + group % 2


def piece_of(weight, piece, columns):
    step, half = piece
    place = jnp.bitwise_xor(lax.axis_index("tp"), step_mask(lax.axis_index("group"), step))
    depth = weight.shape[0] // 2
    return weight.at[
        pl.ds(half * depth, depth), pl.ds(pl.multiple_of(place * columns, columns), columns)
    ]


def fetch(weight, pieces, targets, sems, columns):
    copies = [
        pltpu.make_async_copy(piece_of(weight, piece, columns), target, sems.at[i])
        for i, (piece, target) in enumerate(zip(pieces, targets))
    ]

    for copy in copies:
        copy.start()
    return copies


def region(body):
    pl.when(lax.axis_index("group") >= 0)(body)


def fetch_kernel(weight, _, *rest, pieces, columns):
    for copy in fetch(weight, pieces, rest[:-1], rest[-1], columns):
        copy.wait()


def slot_kernel(*refs, groups, rows, heads, kv_heads, slots, chunk, pieces, columns):
    owners, fills, free = refs[:3]
    shards = refs[3 : 3 + groups]
    keys, values, weight_in = refs[3 + groups : 6 + groups]
    packed, *rest = refs[6 + groups :]
    q_heads, scores, fetch_sems = rest[len(pieces) :]
    weight_copies = fetch(weight_in, pieces, rest, fetch_sems, columns)
    positions = keys.shape[1]
    me = lax.axis_index("group")
    row_at = lax.broadcasted_iota(jnp.int32, (rows, heads * HEAD_DIM), 0)
    for s in range(slots):
        owner = jnp.maximum(owners[s], 0)
        home = lax.div(owner, rows)
        row = lax.rem(owner, rows)
        for k in range(groups):

            @pl.when(jnp.bitwise_xor(home, me) == k)
            def _(k=k, s=s, row=row):
                block = jnp.where(row_at == row, shards[k][...].astype(f32), 0.0)
                single = jnp.sum(block, axis=0, keepdims=True)
                for h in range(heads):
                    q_heads[s * heads + h : s * heads + h + 1, :] = single[
                        :, h * HEAD_DIM : (h + 1) * HEAD_DIM
                    ]

    place = lax.broadcasted_iota(jnp.int32, (heads, positions), 1)
    lane = lax.broadcasted_iota(jnp.int32, (heads, LANES), 1)
    stats = jnp.where(lane == 3 * slots, free[0].astype(f32), 0.0)
    for s in range(slots):
        at = pl.ds(s * heads, heads)
        query = spread_heads(q_heads[at, :].astype(bf16), kv_heads)
        for c in range(0, positions, chunk):
            scores[at, c : c + chunk] = scores_of(query, keys[s, c : c + chunk, :])
    for s in range(slots):
        at = pl.ds(s * heads, heads)
        visible = place < fills[s]
        masked = jnp.where(visible, scores[at, :], far_below)
        high = jnp.max(masked, axis=-1, keepdims=True)
        weights = jnp.where(visible, jnp.exp(masked - high), 0.0)
        total = jnp.sum(weights, axis=-1, keepdims=True)
        mixed = jnp.dot(weights.astype(bf16), values[s], preferred_element_type=f32)
        packed[at, :] = own_columns(mixed, kv_heads)
        stats = jnp.where(lane == s, high, stats)
        stats = jnp.where(lane == slots + s, total, stats)
        stats = jnp.where(lane == 2 * slots + s, owners[s].astype(f32), stats)
    packed[slots * heads :, :] = stats
    for copy in weight_copies:
        copy.wait()


def project(x, halves, same, other, chunk, own=None):
    rows, depth = x.shape[0] // 2, x.shape[1] // 2
    for c in range(0, same.shape[1], chunk):
        at = slice(c, c + chunk)
        product = jnp.dot(
            x[:, :depth], halves[0][:, at], preferred_element_type=f32
        ) + jnp.dot(x[:, depth:], halves[1][:, at], preferred_element_type=f32)
        same[:, at] = product[:rows].astype(same.dtype)
        other[:, at] = product[rows:].astype(other.dtype)
        if own is not None:
            own[:, at] = product[:rows]


def combine_kernel(*refs, groups, rows, heads, slots, pieces, last, columns, chunk):
    local, gathered, halves = refs[:2], refs[2 : 2 + groups], refs[2 + groups : 4 + groups]
    weight_in, x_ref, free_total, same, other, *rest = refs[4 + groups :]
    own = rest.pop(0) if last else None
    mixed, high, total, sems = rest[len(pieces) :]
    copies = fetch(weight_in, pieces, rest, sems, columns)

    @region
    def _():
        flat, each = rows * heads, (slots + 1) * heads
        me = lax.axis_index("group")
        first, second = me * rows, jnp.bitwise_xor(me, 1) * rows
        free = jnp.zeros((heads, LANES), f32)
        found = []
        for part in gathered:
            for k in range(0, part.shape[0], each):
                stats = part[k + slots * heads : k + each, :]
                free = free + stats
                for s in range(slots):
                    owner = stats[0, 2 * slots + s].astype(jnp.int32)
                    found.append((part, k, s, stats, owner))
        free_total[0] = free[0, 3 * slots].astype(jnp.int32)
        for i in range(2):
            stats = local[i][flat:, :]
            high[i * flat : (i + 1) * flat, :] = jnp.broadcast_to(stats[:, 0:1], (flat, LANES))
        slot_stats = []
        for part, k, s, stats, owner in found:
            in_first = (owner >= first) & (owner < first + rows)
            in_second = (owner >= second) & (owner < second + rows)
            row = jnp.where(
                in_first, owner - first, jnp.where(in_second, owner - second + rows, 0)
            )
            mine = in_first | in_second
            at = pl.ds(pl.multiple_of(row * heads, heads), heads)
            slot_high = jnp.broadcast_to(stats[:, s : s + 1], (heads, LANES))
            slot_total = jnp.broadcast_to(stats[:, slots + s : slots + s + 1], (heads, LANES))
            slot_stats.append((part, k + s * heads, mine, at, slot_high, slot_total))
            high[at, :] = jnp.maximum(high[at, :], jnp.where(mine, slot_high, far_below))
        for i in range(2):
            at = slice(i * flat, (i + 1) * flat)
            stats = local[i][flat:, :]
            keep = jnp.exp(jnp.broadcast_to(stats[:, 0:1], (flat, LANES)) - high[at, :])
            mixed[at, :] = keep * local[i][:flat, :]
            total[at, :] = keep * jnp.broadcast_to(stats[:, 1:2], (flat, LANES))
        for part, k, mine, at, slot_high, slot_total in slot_stats:
            add = jnp.where(mine, jnp.exp(jnp.minimum(slot_high - high[at, :], 0.0)), 0.0)
            mixed[at, :] = mixed[at, :] + add * part[k : k + heads, :]
            total[at, :] = total[at, :] + add * slot_total
        mixed[...] = mixed[...] / total[...]
        for h in range(heads):
            x_ref[:, h * HEAD_DIM : (h + 1) * HEAD_DIM] = mixed[
                pl.ds(h, 2 * rows, stride=heads), :
            ].astype(bf16)

    @region
    def _():
        project(x_ref[...], halves, same, other, chunk, own)

    for copy in copies:
        copy.wait()


def project_kernel(x_ref, *refs, pieces, last, columns, chunk):
    halves = refs[:2]
    weight_in, same, other, *rest = refs[2:]
    own = rest.pop(0) if last else None
    copies = fetch(weight_in, pieces, rest, rest[-1], columns)
    region(lambda: project(x_ref[...], halves, same, other, chunk, own))
    for copy in copies:
        copy.wait()


def pick_kernel(even, odd, out):
    first = lax.axis_index("group") % 2 == 0

    @pl.when(first)
    def _():
        out[...] = even[...]

    @pl.when(jnp.logical_not(first))
    def _():
        out[...] = odd[...]


def sum_kernel(own, crossed, *refs):
    total = jnp.where(lax.axis_index("group") % 2 == 0, own[...], crossed[...].astype(f32))
    for part in refs[:-1]:
        total = total + part[...].astype(f32)
    refs[-1][...] = total.astype(bf16)


def send_block(value, step, crossed):
    groups, tp = lax.axis_size("group"), lax.axis_size("tp")
    pairs = [
        (g * tp + z, g * tp + (z ^ step_mask(g ^ crossed, step)))
        for g in range(groups)
        for z in range(tp)
    ]
    return lax.ppermute(value, ("group", "tp"), pairs)


def swap(value, axis, mask):
    size = lax.axis_size(axis)
    return lax.ppermute(value, axis, [(i, i ^ mask) for i in range(size)])


def gather_group(value):
    groups = lax.axis_size("group")
    found = [None] * groups
    found[0] = value
    found[1] = swap(value, "group", 1)
    for k in range(2, groups, 2):
        found[k] = swap(value, "group", k)
    for k in range(2, groups, 2):
        found[k + 1] = swap(found[k], "group", 1)
    return found


def step(
    queries,
    cache_keys,
    cache_values,
    pool_keys,
    pool_values,
    row_lengths,
    slot_owner,
    slot_fill,
    free_counts,
    out_weight,
):
    groups, tp = lax.axis_size("group"), lax.axis_size("tp")
    rows, width = queries.shape
    heads = width // HEAD_DIM
    kv_heads = cache_keys.shape[2] // HEAD_DIM
    slots, positions = pool_keys.shape[:2]
    columns = out_weight.shape[1] // tp
    chunk = math.gcd(columns, 512)
    sizes = dict(rows=rows, heads=heads)

    shards = gather_group(queries)
    out_weight = pltpu.with_memory_space_constraint(out_weight, pltpu.MemorySpace.HBM)
    copies = pltpu.SemaphoreType.DMA

    order = list(range(tp // 2 - 1, -1, -1))
    pieces = [(step, half) for step in order for half in range(2)]
    held = jax.ShapeDtypeStruct((width // 2, columns), out_weight.dtype)
    piece_bytes = width * columns
    weights = {}

    def take(count):
        taken = pieces[:count]
        del pieces[:count]
        return taken

    token = call(open_kernel, jax.ShapeDtypeStruct((8, LANES), f32), [HBM], vmem=1 << 20)(
        out_weight
    )
    taken = take(1)
    local, *more = call(
        lambda *refs, taken=taken: local_kernel(
            *refs, kv_heads=kv_heads, pieces=taken, columns=columns, **sizes
        ),
        [
            jax.ShapeDtypeStruct((2 * rows * heads, LANES), f32),
        ]
        + [held] * len(taken),
        [SMEM, VMEM, VMEM, VMEM, HBM, VMEM],
        scratch=[
            pltpu.VMEM((rows * heads, HEAD_DIM), f32),
            pltpu.VMEM((rows * heads, cache_keys.shape[1]), f32),
            pltpu.VMEM((rows, heads, cache_keys.shape[1]), bf16),
            copies((1,)),
        ],
        moved=2 * (cache_keys.size + cache_values.size),
        vmem=4 << 20,
    )(row_lengths, queries, cache_keys, cache_values, out_weight, token)
    weights.update(zip(taken, more))
    pair_local = swap(local, "group", 1)

    taken = take(1)
    packed, *more = call(
        lambda *refs, taken=taken: slot_kernel(
            *refs,
            groups=groups,
            kv_heads=kv_heads,
            slots=slots,
            chunk=math.gcd(positions, 512),
            pieces=taken,
            columns=columns,
            **sizes,
        ),
        [jax.ShapeDtypeStruct(((slots + 1) * heads, LANES), f32)] + [held] * len(taken),
        [SMEM] * 3 + [VMEM] * (groups + 2) + [HBM],
        scratch=[
            pltpu.VMEM((slots * heads, HEAD_DIM), f32),
            pltpu.VMEM((slots * heads, positions), f32),
            copies((1,)),
        ],
        moved=2 * (pool_keys.size + pool_values.size),
        vmem=4 << 20,
    )(slot_owner, slot_fill, free_counts, *shards, pool_keys, pool_values, out_weight)
    weights.update(zip(taken, more))

    far = gather_group(packed)
    taken = take(1)
    more = call(
        lambda *refs, taken=taken: fetch_kernel(*refs, pieces=taken, columns=columns),
        [held] * len(taken),
        [HBM, pl.BlockSpec(memory_space=pl.ANY)],
        scratch=[copies((1,))],
        moved=piece_bytes,
        vmem=1 << 20,
    )(out_weight, packed)
    weights.update(zip(taken, more))

    block = jax.ShapeDtypeStruct((rows, columns), bf16)
    whole = jax.ShapeDtypeStruct((rows, columns), f32)
    received = []
    for i, step in enumerate(order):
        last = step == 0
        taken = take(max(0, len(pieces) - 2 * (len(order) - 2 - i)))
        outs = [block] * 2 + [whole] * last + [held] * len(taken)
        settings = dict(pieces=taken, last=last, columns=columns, chunk=chunk)
        halves = [weights[step, half] for half in range(2)]
        moved = piece_bytes * max(2, len(taken))
        if i == 0:
            x, free_total, same, other, *more = call(
                lambda *refs: combine_kernel(
                    *refs, groups=groups, slots=slots, **settings, **sizes
                ),
                [
                    jax.ShapeDtypeStruct((2 * rows, width), bf16),
                    jax.ShapeDtypeStruct((1,), jnp.int32),
                ]
                + outs,
                [VMEM] * (4 + groups) + [HBM],
                out_specs=[VMEM, SMEM] + [VMEM] * len(outs),
                scratch=[pltpu.VMEM((2 * rows * heads, LANES), f32)] * 3
                + [copies((max(1, len(taken)),))],
                moved=moved,
            )(local, pair_local, *far, *halves, out_weight)
        else:
            same, other, *more = call(
                lambda *refs, settings=settings: project_kernel(*refs, **settings),
                outs,
                [VMEM] * 3 + [HBM],
                scratch=[copies((max(1, len(taken)),))],
                moved=moved,
                vmem=4 << 20,
            )(x, *halves, out_weight)
        if last:
            own = more.pop(0)
        weights.update(zip(taken, more))
        crossed = swap(other, "group", 1)
        if last:
            leaving = call(pick_kernel, block, [VMEM] * 2, vmem=1 << 20)(crossed, same)
            received.append(swap(leaving, "tp", 1))
        else:
            received.append(send_block(same, step, 0))
            received.append(send_block(crossed, step, 1))
    mixed_out = call(sum_kernel, block, [VMEM] * (2 + len(received)))(own, crossed, *received)
    return (mixed_out, free_total)


def solution(mesh):
    in_specs = (
        P("group", "tp"),
        P("group", None, "tp"),
        P("group", None, "tp"),
        P("group", None, "tp"),
        P("group", None, "tp"),
        P("group"),
        P("group"),
        P("group"),
        P("group"),
        P("tp", None),
    )
    out_specs = (P("group", "tp"), P())
    return jax.shard_map(step, mesh=mesh, in_specs=in_specs, out_specs=out_specs, check_vma=False)
```

```python
import math

import jax
import jax.numpy as jnp
from jax import lax
from jax.experimental import pallas as pl
from jax.experimental.pallas import tpu as pltpu
from jax.sharding import PartitionSpec as P


HEAD_DIM = 128
LANES = 128
PARTS = 4
far_below = -1e30


VMEM = pl.BlockSpec(memory_space=pltpu.VMEM)
SMEM = pl.BlockSpec(memory_space=pltpu.SMEM)
HBM = pl.BlockSpec(memory_space=pltpu.MemorySpace.HBM)
f32 = jnp.float32
bf16 = jnp.bfloat16


def call(kernel, outs, ins, scratch=(), out_specs=None, flops=0, moved=0, vmem=8 << 20):
    return pl.pallas_call(
        kernel,
        out_shape=outs,
        in_specs=ins,
        out_specs=out_specs if out_specs is not None else jax.tree.map(lambda _: VMEM, outs),
        scratch_shapes=scratch,
        cost_estimate=pl.CostEstimate(flops=flops, bytes_accessed=moved, transcendentals=0),
        compiler_params=pltpu.CompilerParams(vmem_limit_bytes=vmem),
    )


def spread_heads(tile, kv_heads):
    if kv_heads == 1:
        return tile
    heads = tile.shape[0]
    owner = lax.broadcasted_iota(jnp.int32, tile.shape, 0) // (heads // kv_heads)
    return jnp.concatenate(
        [jnp.where(owner == k, tile, jnp.zeros_like(tile)) for k in range(kv_heads)], axis=1
    )


def own_columns(wide, kv_heads):
    if kv_heads == 1:
        return wide
    heads = wide.shape[0]
    owner = lax.broadcasted_iota(jnp.int32, (heads, HEAD_DIM), 0) // (heads // kv_heads)
    picked = wide[:, :HEAD_DIM]
    for k in range(1, kv_heads):
        picked = jnp.where(owner == k, wide[:, k * HEAD_DIM : (k + 1) * HEAD_DIM], picked)
    return picked


def scores_of(query, keys):
    return lax.dot_general(
        query, keys, (((1,), (1,)), ((), ())), preferred_element_type=f32
    ) * (math.log2(math.e) / math.sqrt(HEAD_DIM))


def open_kernel(_, token):
    token[...] = jnp.zeros_like(token)


def local_kernel(
    lengths, q_ref, keys, values, weight_in, _, packed, *rest,
    rows, heads, kv_heads, pieces, columns,
):
    q_heads, scores, weights, fetch_sems = rest[len(pieces) :]
    positions = keys.shape[1]
    weight_copies = fetch(weight_in, pieces, rest, fetch_sems, columns)

    @region
    def _():
        wide = q_ref[...].astype(f32)
        for h in range(heads):
            q_heads[pl.ds(h, rows, stride=heads), :] = wide[:, h * HEAD_DIM : (h + 1) * HEAD_DIM]

    place = lax.broadcasted_iota(jnp.int32, (heads, positions), 1)

    def score(r):
        query = spread_heads(q_heads[pl.ds(r * heads, heads), :].astype(bf16), kv_heads)
        scores[r] = jnp.where(place < lengths[r], scores_of(query, keys[r]), far_below)

    def weigh(r):
        high = jnp.max(scores[r], axis=-1, keepdims=True)
        weight = jnp.exp2(scores[r] - high)
        total = jnp.sum(weight, axis=-1, keepdims=True)
        weights[r] = weight.astype(bf16)
        for i, value in ((1, high), (2, total)):
            at = pl.ds((i * rows + r) * heads, heads)
            packed[at, :] = jnp.broadcast_to(value, (heads, LANES))

    def mix(r):
        mixed = jnp.dot(weights[r], values[r], preferred_element_type=f32)
        packed[pl.ds(r * heads, heads), :] = own_columns(mixed, kv_heads)

    @region
    def _():
        pipeline((score, weigh, mix), rows, 3)

    for copy in weight_copies:
        copy.wait()


def pipeline(stages, count, apart):
    for t in range(count + apart * (len(stages) - 1)):
        for k, stage in enumerate(stages):
            if 0 <= t - k * apart < count:
                stage(t - k * apart)


def step_mask(group, step):
    return 2 * step + group % 2


def piece_of(weight, piece, columns):
    step, part = piece
    place = jnp.bitwise_xor(lax.axis_index("tp"), step_mask(lax.axis_index("group"), step))
    depth = weight.shape[0] // PARTS
    return weight.at[
        pl.ds(part * depth, depth), pl.ds(pl.multiple_of(place * columns, columns), columns)
    ]


def fetch(weight, pieces, targets, sems, columns):
    copies = [
        pltpu.make_async_copy(piece_of(weight, piece, columns), target, sems.at[i])
        for i, (piece, target) in enumerate(zip(pieces, targets))
    ]

    for copy in copies:
        copy.start()
    return copies


def region(body):
    pl.when(lax.axis_index("group") >= 0)(body)


def fetch_kernel(weight, _, *rest, pieces, columns):
    for copy in fetch(weight, pieces, rest[:-1], rest[-1], columns):
        copy.wait()


def split_stats(stats):
    spread = jnp.zeros_like(stats)
    for i in range(3):
        term = stats.astype(bf16).astype(f32)
        stats = stats - term
        spread = spread + (pltpu.roll(term, i * LANES // 4, 1) if i else term)
    return spread.astype(bf16)


def join_stats(tile):
    spread = tile.astype(f32)
    return (
        spread + pltpu.roll(spread, 3 * LANES // 4, 1) + pltpu.roll(spread, 2 * LANES // 4, 1)
    )


def slot_kernel(*refs, groups, rows, heads, kv_heads, slots, chunk, pieces, columns):
    owners, fills, free = refs[:3]
    shards = refs[3 : 3 + groups]
    keys, values, weight_in = refs[3 + groups : 6 + groups]
    packed, *rest = refs[6 + groups :]
    q_heads, scores, weights, fetch_sems = rest[len(pieces) :]
    weight_copies = fetch(weight_in, pieces, rest, fetch_sems, columns)
    positions = keys.shape[1]
    me = lax.axis_index("group")
    row_at = lax.broadcasted_iota(jnp.int32, (rows, heads * HEAD_DIM), 0)
    for s in range(slots):
        owner = jnp.maximum(owners[s], 0)
        home = lax.div(owner, rows)
        row = lax.rem(owner, rows)
        for k in range(groups):

            @pl.when(jnp.bitwise_xor(home, me) == k)
            def _(k=k, s=s, row=row):
                block = jnp.where(row_at == row, shards[k][...].astype(f32), 0.0)
                single = jnp.sum(block, axis=0, keepdims=True)
                for h in range(heads):
                    q_heads[s * heads + h : s * heads + h + 1, :] = single[
                        :, h * HEAD_DIM : (h + 1) * HEAD_DIM
                    ]

    lane = lax.broadcasted_iota(jnp.int32, (heads, LANES), 1)
    stats = jnp.where(lane == 3 * slots, free[0].astype(f32), 0.0)
    places = lax.broadcasted_iota(jnp.int32, (heads, chunk), 1)
    queries = [
        spread_heads(q_heads[s * heads : (s + 1) * heads, :].astype(bf16), kv_heads)
        for s in range(slots)
    ]
    highs, bases = [None] * slots, [None] * slots
    totals, mixes = [0.0] * slots, [0.0] * slots
    steps = positions // chunk

    def score(s, c):
        at = pl.ds(c * chunk, chunk)
        found = jnp.where(
            places < fills[s] - c * chunk, scores_of(queries[s], keys[s, at, :]), far_below
        )
        scores[s, :, at] = found
        highs[s] = found if c == 0 else jnp.maximum(highs[s], found)
        if c == steps - 1:
            highs[s] = jnp.max(highs[s], axis=-1, keepdims=True)
            bases[s] = jnp.maximum(highs[s], far_below / 2)

    def weigh(s, c):
        at = pl.ds(c * chunk, chunk)
        weight = jnp.exp2(scores[s, :, at] - bases[s])
        totals[s] = totals[s] + weight
        weights[s, :, at] = weight.astype(bf16)

    def mix(s, c):
        at = pl.ds(c * chunk, chunk)
        mixes[s] = mixes[s] + jnp.dot(
            weights[s, :, at], values[s, at, :], preferred_element_type=f32
        )

    for t in range(slots + 2):
        for c in range(steps):
            for stage, s in ((score, t), (weigh, t - 1), (mix, t - 2)):
                if 0 <= s < slots:
                    stage(s, c)
    for s in range(slots):
        total = jnp.sum(totals[s], axis=-1, keepdims=True)
        packed[s * heads : (s + 1) * heads, :] = own_columns(mixes[s], kv_heads).astype(bf16)
        stats = jnp.where(lane == s, highs[s], stats)
        stats = jnp.where(lane == slots + s, total, stats)
        stats = jnp.where(lane == 2 * slots + s, owners[s].astype(f32), stats)
    packed[slots * heads :, :] = split_stats(stats)
    for copy in weight_copies:
        copy.wait()


def project(x, held, same, other, chunk, own=None):
    rows, depth = x.shape[0] // 2, x.shape[1] // PARTS
    for c in range(0, same.shape[1], chunk):
        at = slice(c, c + chunk)
        product = sum(
            jnp.dot(
                x[:, p * depth : (p + 1) * depth], held[p][:, at], preferred_element_type=f32
            )
            for p in range(PARTS)
        )
        same[:, at] = product[:rows].astype(same.dtype)
        other[:, at] = product[rows:].astype(other.dtype)
        if own is not None:
            own[:, at] = product[:rows]


def combine_kernel(*refs, groups, rows, heads, slots, pieces, last, columns, chunk):
    local, gathered = refs[:2], refs[2 : 2 + groups]
    held, refs = refs[2 + groups : 2 + groups + PARTS], refs[2 + groups + PARTS :]
    weight_in, x_ref, free_total, same, other, *rest = refs
    own = rest.pop(0) if last else None
    mixed, high, total, sems = rest[len(pieces) :]
    copies = fetch(weight_in, pieces, rest, sems, columns)

    @region
    def _():
        flat, each = rows * heads, (slots + 1) * heads
        me = lax.axis_index("group")
        first, second = me * rows, jnp.bitwise_xor(me, 1) * rows
        free = jnp.zeros((heads, LANES), f32)
        found = []
        for part in gathered:
            for k in range(0, part.shape[0], each):
                stats = join_stats(part[k + slots * heads : k + each, :])
                free = free + stats
                for s in range(slots):
                    owner = stats[0, 2 * slots + s].astype(jnp.int32)
                    found.append((part, k, s, stats, owner))
        free_total[0] = free[0, 3 * slots].astype(jnp.int32)
        for i in range(2):
            high[i * flat : (i + 1) * flat, :] = local[i][flat : 2 * flat, :]
        slot_stats = []
        for part, k, s, stats, owner in found:
            in_first = (owner >= first) & (owner < first + rows)
            in_second = (owner >= second) & (owner < second + rows)
            row = jnp.where(
                in_first, owner - first, jnp.where(in_second, owner - second + rows, 0)
            )
            mine = in_first | in_second
            at = pl.ds(pl.multiple_of(row * heads, heads), heads)
            slot_high = jnp.broadcast_to(stats[:, s : s + 1], (heads, LANES))
            slot_total = jnp.broadcast_to(stats[:, slots + s : slots + s + 1], (heads, LANES))
            slot_stats.append((part, k + s * heads, mine, at, slot_high, slot_total))
            high[at, :] = jnp.maximum(high[at, :], jnp.where(mine, slot_high, far_below))
        for i in range(2):
            at = slice(i * flat, (i + 1) * flat)
            keep = jnp.exp2(local[i][flat : 2 * flat, :] - high[at, :])
            mixed[at, :] = keep * local[i][:flat, :]
            total[at, :] = keep * local[i][2 * flat :, :]
        for part, k, mine, at, slot_high, slot_total in slot_stats:
            add = jnp.where(mine, jnp.exp2(jnp.minimum(slot_high - high[at, :], 0.0)), 0.0)
            mixed[at, :] = mixed[at, :] + add * part[k : k + heads, :].astype(f32)
            total[at, :] = total[at, :] + add * slot_total
        mixed[...] = mixed[...] / total[...]
        for h in range(heads):
            x_ref[:, h * HEAD_DIM : (h + 1) * HEAD_DIM] = mixed[
                pl.ds(h, 2 * rows, stride=heads), :
            ].astype(bf16)

    @region
    def _():
        project(x_ref[...], held, same, other, chunk, own)

    for copy in copies:
        copy.wait()


def project_kernel(x_ref, *refs, pieces, last, columns, chunk):
    held = refs[:PARTS]
    weight_in, same, other, *rest = refs[PARTS:]
    own = rest.pop(0) if last else None
    copies = fetch(weight_in, pieces, rest, rest[-1], columns)
    region(lambda: project(x_ref[...], held, same, other, chunk, own))
    for copy in copies:
        copy.wait()


def pick_kernel(even, odd, out):
    first = lax.axis_index("group") % 2 == 0

    @pl.when(first)
    def _():
        out[...] = even[...]

    @pl.when(jnp.logical_not(first))
    def _():
        out[...] = odd[...]


def sum_kernel(own, crossed, *refs):
    total = jnp.where(lax.axis_index("group") % 2 == 0, own[...], crossed[...].astype(f32))
    for part in refs[:-1]:
        total = total + part[...].astype(f32)
    refs[-1][...] = total.astype(bf16)


def send_block(value, step, crossed):
    groups, tp = lax.axis_size("group"), lax.axis_size("tp")
    pairs = [
        (g * tp + z, g * tp + (z ^ step_mask(g ^ crossed, step)))
        for g in range(groups)
        for z in range(tp)
    ]
    return lax.ppermute(value, ("group", "tp"), pairs)


def swap(value, axis, mask):
    size = lax.axis_size(axis)
    return lax.ppermute(value, axis, [(i, i ^ mask) for i in range(size)])


def gather_group(value):
    groups = lax.axis_size("group")
    found = [None] * groups
    found[0] = value
    found[1] = swap(value, "group", 1)
    for k in range(2, groups, 2):
        found[k] = swap(value, "group", k)
    for k in range(2, groups, 2):
        found[k + 1] = swap(found[k], "group", 1)
    return found


def step(
    queries,
    cache_keys,
    cache_values,
    pool_keys,
    pool_values,
    row_lengths,
    slot_owner,
    slot_fill,
    free_counts,
    out_weight,
):
    groups, tp = lax.axis_size("group"), lax.axis_size("tp")
    rows, width = queries.shape
    heads = width // HEAD_DIM
    kv_heads = cache_keys.shape[2] // HEAD_DIM
    slots, positions = pool_keys.shape[:2]
    columns = out_weight.shape[1] // tp
    chunk = math.gcd(columns, 512)
    sizes = dict(rows=rows, heads=heads)

    shards = gather_group(queries)
    out_weight = pltpu.with_memory_space_constraint(out_weight, pltpu.MemorySpace.HBM)
    copies = pltpu.SemaphoreType.DMA

    order = list(range(tp // 2 - 1, -1, -1))
    pieces = [(step, part) for step in order for part in range(PARTS)]
    held = jax.ShapeDtypeStruct((width // PARTS, columns), out_weight.dtype)
    piece_bytes = 2 * width * columns // PARTS
    weights = {}

    def take(count):
        taken = pieces[:count]
        del pieces[:count]
        return taken

    token = call(open_kernel, jax.ShapeDtypeStruct((8, LANES), f32), [HBM], vmem=1 << 20)(
        out_weight
    )
    taken = take(0)
    local, *more = call(
        lambda *refs, taken=taken: local_kernel(
            *refs, kv_heads=kv_heads, pieces=taken, columns=columns, **sizes
        ),
        [
            jax.ShapeDtypeStruct((3 * rows * heads, LANES), f32),
        ]
        + [held] * len(taken),
        [SMEM, VMEM, VMEM, VMEM, HBM, VMEM],
        scratch=[
            pltpu.VMEM((rows * heads, HEAD_DIM), f32),
            pltpu.VMEM((rows, heads, cache_keys.shape[1]), f32),
            pltpu.VMEM((rows, heads, cache_keys.shape[1]), bf16),
            copies((1,)),
        ],
        moved=2 * (cache_keys.size + cache_values.size),
        vmem=4 << 20,
    )(row_lengths, queries, cache_keys, cache_values, out_weight, token)
    weights.update(zip(taken, more))
    pair_local = swap(local, "group", 1)

    taken = take(3)
    packed, *more = call(
        lambda *refs, taken=taken: slot_kernel(
            *refs,
            groups=groups,
            kv_heads=kv_heads,
            slots=slots,
            chunk=math.gcd(positions, 512),
            pieces=taken,
            columns=columns,
            **sizes,
        ),
        [jax.ShapeDtypeStruct(((slots + 1) * heads, LANES), bf16)] + [held] * len(taken),
        [SMEM] * 3 + [VMEM] * (groups + 2) + [HBM],
        scratch=[
            pltpu.VMEM((slots * heads, HEAD_DIM), f32),
            pltpu.VMEM((slots, heads, positions), f32),
            pltpu.VMEM((slots, heads, positions), bf16),
            copies((len(taken),)),
        ],
        moved=2 * (pool_keys.size + pool_values.size),
        vmem=4 << 20,
    )(slot_owner, slot_fill, free_counts, *shards, pool_keys, pool_values, out_weight)
    weights.update(zip(taken, more))

    far = gather_group(packed)
    taken = take(2)
    more = call(
        lambda *refs, taken=taken: fetch_kernel(*refs, pieces=taken, columns=columns),
        [held] * len(taken),
        [HBM, pl.BlockSpec(memory_space=pl.ANY)],
        scratch=[copies((len(taken),))],
        moved=piece_bytes * len(taken),
        vmem=1 << 20,
    )(out_weight, packed)
    weights.update(zip(taken, more))

    block = jax.ShapeDtypeStruct((rows, columns), bf16)
    whole = jax.ShapeDtypeStruct((rows, columns), f32)
    received = []
    for i, step in enumerate(order):
        last = step == 0
        taken = take(max(0, len(pieces) - PARTS * (len(order) - 2 - i)))
        outs = [block] * 2 + [whole] * last + [held] * len(taken)
        settings = dict(pieces=taken, last=last, columns=columns, chunk=chunk)
        ready = [weights[step, part] for part in range(PARTS)]
        moved = piece_bytes * max(PARTS, len(taken))
        if i == 0:
            x, free_total, same, other, *more = call(
                lambda *refs: combine_kernel(
                    *refs, groups=groups, slots=slots, **settings, **sizes
                ),
                [
                    jax.ShapeDtypeStruct((2 * rows, width), bf16),
                    jax.ShapeDtypeStruct((1,), jnp.int32),
                ]
                + outs,
                [VMEM] * (2 + groups + PARTS) + [HBM],
                out_specs=[VMEM, SMEM] + [VMEM] * len(outs),
                scratch=[pltpu.VMEM((2 * rows * heads, LANES), f32)] * 3
                + [copies((max(1, len(taken)),))],
                moved=moved,
            )(local, pair_local, *far, *ready, out_weight)
        else:
            same, other, *more = call(
                lambda *refs, settings=settings: project_kernel(*refs, **settings),
                outs,
                [VMEM] * (1 + PARTS) + [HBM],
                scratch=[copies((max(1, len(taken)),))],
                moved=moved,
                vmem=4 << 20,
            )(x, *ready, out_weight)
        if last:
            own = more.pop(0)
        weights.update(zip(taken, more))
        crossed = swap(other, "group", 1)
        if last:
            leaving = call(pick_kernel, block, [VMEM] * 2, vmem=1 << 20)(crossed, same)
            received.append(swap(leaving, "tp", 1))
        else:
            received.append(send_block(same, step, 0))
            received.append(send_block(crossed, step, 1))
    mixed_out = call(sum_kernel, block, [VMEM] * (2 + len(received)))(own, crossed, *received)
    return (mixed_out, free_total)


def solution(mesh):
    in_specs = (
        P("group", "tp"),
        P("group", None, "tp"),
        P("group", None, "tp"),
        P("group", None, "tp"),
        P("group", None, "tp"),
        P("group"),
        P("group"),
        P("group"),
        P("group"),
        P("tp", None),
    )
    out_specs = (P("group", "tp"), P())
    return jax.shard_map(step, mesh=mesh, in_specs=in_specs, out_specs=out_specs, check_vma=False)
```

```python
import math

import jax
import jax.numpy as jnp
from jax import lax
from jax.experimental import pallas as pl
from jax.experimental.pallas import tpu as pltpu
from jax.sharding import PartitionSpec as P


HEAD_DIM = 128
LANES = 128
far_below = -1e30


VMEM = pl.BlockSpec(memory_space=pltpu.VMEM)
SMEM = pl.BlockSpec(memory_space=pltpu.SMEM)
HBM = pl.BlockSpec(memory_space=pltpu.MemorySpace.HBM)
f32 = jnp.float32
bf16 = jnp.bfloat16


def call(kernel, outs, ins, scratch=(), out_specs=None, flops=0, moved=0, vmem=8 << 20):
    return pl.pallas_call(
        kernel,
        out_shape=outs,
        in_specs=ins,
        out_specs=out_specs if out_specs is not None else jax.tree.map(lambda _: VMEM, outs),
        scratch_shapes=scratch,
        cost_estimate=pl.CostEstimate(flops=flops, bytes_accessed=moved, transcendentals=0),
        compiler_params=pltpu.CompilerParams(vmem_limit_bytes=vmem),
    )


def spread_heads(tile, kv_heads):
    if kv_heads == 1:
        return tile
    heads = tile.shape[0]
    owner = lax.broadcasted_iota(jnp.int32, tile.shape, 0) // (heads // kv_heads)
    return jnp.concatenate(
        [jnp.where(owner == k, tile, jnp.zeros_like(tile)) for k in range(kv_heads)], axis=1
    )


def own_columns(wide, kv_heads):
    if kv_heads == 1:
        return wide
    heads = wide.shape[0]
    owner = lax.broadcasted_iota(jnp.int32, (heads, HEAD_DIM), 0) // (heads // kv_heads)
    picked = wide[:, :HEAD_DIM]
    for k in range(1, kv_heads):
        picked = jnp.where(owner == k, wide[:, k * HEAD_DIM : (k + 1) * HEAD_DIM], picked)
    return picked


def scores_of(query, keys):
    return lax.dot_general(
        query, keys, (((1,), (1,)), ((), ())), preferred_element_type=f32
    ) * (math.log2(math.e) / math.sqrt(HEAD_DIM))


def open_kernel(_, token):
    token[...] = jnp.zeros_like(token)


def local_kernel(
    lengths, q_ref, keys, values, weight_in, _, packed, *rest,
    rows, heads, kv_heads, pieces, columns,
):
    q_heads, scores, weights, fetch_sems = rest[len(pieces) :]
    positions = keys.shape[1]
    weight_copies = fetch(weight_in, pieces, rest, fetch_sems, columns)

    @region
    def _():
        wide = q_ref[...].astype(f32)
        for h in range(heads):
            q_heads[pl.ds(h, rows, stride=heads), :] = wide[:, h * HEAD_DIM : (h + 1) * HEAD_DIM]

    place = lax.broadcasted_iota(jnp.int32, (heads, positions), 1)

    def score(r):
        query = spread_heads(q_heads[pl.ds(r * heads, heads), :].astype(bf16), kv_heads)
        scores[r] = jnp.where(place < lengths[r], scores_of(query, keys[r]), far_below)

    def weigh(r):
        high = jnp.max(scores[r], axis=-1, keepdims=True)
        weight = jnp.exp2(scores[r] - high)
        total = jnp.sum(weight, axis=-1, keepdims=True)
        weights[r] = weight.astype(bf16)
        for i, value in ((1, high), (2, total)):
            at = pl.ds((i * rows + r) * heads, heads)
            packed[at, :] = jnp.broadcast_to(value, (heads, LANES))

    def mix(r):
        mixed = jnp.dot(weights[r], values[r], preferred_element_type=f32)
        packed[pl.ds(r * heads, heads), :] = own_columns(mixed, kv_heads)

    @region
    def _():
        pipeline((score, weigh, mix), rows, 4)

    for copy in weight_copies:
        copy.wait()


def pipeline(stages, count, apart):
    for t in range(count + apart * (len(stages) - 1)):
        for k, stage in enumerate(stages):
            if 0 <= t - k * apart < count:
                stage(t - k * apart)


def step_mask(group, step):
    return 2 * step + group % 2


def piece_of(weight, piece, columns):
    step, half = piece
    place = jnp.bitwise_xor(lax.axis_index("tp"), step_mask(lax.axis_index("group"), step))
    depth = weight.shape[0] // 2
    return weight.at[
        pl.ds(half * depth, depth), pl.ds(pl.multiple_of(place * columns, columns), columns)
    ]


def fetch(weight, pieces, targets, sems, columns):
    copies = [
        pltpu.make_async_copy(piece_of(weight, piece, columns), target, sems.at[i])
        for i, (piece, target) in enumerate(zip(pieces, targets))
    ]

    for copy in copies:
        copy.start()
    return copies


def region(body):
    pl.when(lax.axis_index("group") >= 0)(body)


def fetch_kernel(weight, _, *rest, pieces, columns):
    for copy in fetch(weight, pieces, rest[:-1], rest[-1], columns):
        copy.wait()


def split_stats(stats):
    spread = jnp.zeros_like(stats)
    for i in range(3):
        term = stats.astype(bf16).astype(f32)
        stats = stats - term
        spread = spread + (pltpu.roll(term, i * LANES // 4, 1) if i else term)
    return spread.astype(bf16)


def join_stats(tile):
    spread = tile.astype(f32)
    return (
        spread + pltpu.roll(spread, 3 * LANES // 4, 1) + pltpu.roll(spread, 2 * LANES // 4, 1)
    )


def slot_kernel(*refs, groups, rows, heads, kv_heads, slots, chunk, pieces, columns):
    owners, fills, free = refs[:3]
    shards = refs[3 : 3 + groups]
    keys, values, weight_in = refs[3 + groups : 6 + groups]
    packed, *rest = refs[6 + groups :]
    q_heads, scores, weights, fetch_sems = rest[len(pieces) :]
    weight_copies = fetch(weight_in, pieces, rest, fetch_sems, columns)
    positions = keys.shape[1]
    me = lax.axis_index("group")
    row_at = lax.broadcasted_iota(jnp.int32, (rows, heads * HEAD_DIM), 0)
    for s in range(slots):
        owner = jnp.maximum(owners[s], 0)
        home = lax.div(owner, rows)
        row = lax.rem(owner, rows)
        for k in range(groups):

            @pl.when(jnp.bitwise_xor(home, me) == k)
            def _(k=k, s=s, row=row):
                block = jnp.where(row_at == row, shards[k][...].astype(f32), 0.0)
                single = jnp.sum(block, axis=0, keepdims=True)
                for h in range(heads):
                    q_heads[s * heads + h : s * heads + h + 1, :] = single[
                        :, h * HEAD_DIM : (h + 1) * HEAD_DIM
                    ]

    lane = lax.broadcasted_iota(jnp.int32, (heads, LANES), 1)
    stats = jnp.where(lane == 3 * slots, free[0].astype(f32), 0.0)
    places = lax.broadcasted_iota(jnp.int32, (heads, chunk), 1)
    queries = [
        spread_heads(q_heads[s * heads : (s + 1) * heads, :].astype(bf16), kv_heads)
        for s in range(slots)
    ]
    highs, bases = [None] * slots, [None] * slots
    totals, mixes = [0.0] * slots, [0.0] * slots
    steps = positions // chunk

    def score(s, c):
        at = pl.ds(c * chunk, chunk)
        found = jnp.where(
            places < fills[s] - c * chunk, scores_of(queries[s], keys[s, at, :]), far_below
        )
        scores[s, :, at] = found
        highs[s] = found if c == 0 else jnp.maximum(highs[s], found)
        if c == steps - 1:
            highs[s] = jnp.max(highs[s], axis=-1, keepdims=True)
            bases[s] = jnp.maximum(highs[s], far_below / 2)

    def weigh(s, c):
        at = pl.ds(c * chunk, chunk)
        weight = jnp.exp2(scores[s, :, at] - bases[s])
        totals[s] = totals[s] + weight
        weights[s, :, at] = weight.astype(bf16)

    def mix(s, c):
        at = pl.ds(c * chunk, chunk)
        mixes[s] = mixes[s] + jnp.dot(
            weights[s, :, at], values[s, at, :], preferred_element_type=f32
        )

    for t in range(slots + 2):
        for c in range(steps):
            for stage, s in ((score, t), (weigh, t - 1), (mix, t - 2)):
                if 0 <= s < slots:
                    stage(s, c)
    for s in range(slots):
        total = jnp.sum(totals[s], axis=-1, keepdims=True)
        packed[s * heads : (s + 1) * heads, :] = own_columns(mixes[s], kv_heads).astype(bf16)
        stats = jnp.where(lane == s, highs[s], stats)
        stats = jnp.where(lane == slots + s, total, stats)
        stats = jnp.where(lane == 2 * slots + s, owners[s].astype(f32), stats)
    packed[slots * heads :, :] = split_stats(stats)
    for copy in weight_copies:
        copy.wait()


def project(x, halves, same, other, chunk, own=None):
    rows, depth = x.shape[0] // 2, x.shape[1] // 2
    for c in range(0, same.shape[1], chunk):
        at = slice(c, c + chunk)
        product = jnp.dot(
            x[:, :depth], halves[0][:, at], preferred_element_type=f32
        ) + jnp.dot(x[:, depth:], halves[1][:, at], preferred_element_type=f32)
        same[:, at] = product[:rows].astype(same.dtype)
        other[:, at] = product[rows:].astype(other.dtype)
        if own is not None:
            own[:, at] = product[:rows]


def combine_kernel(*refs, groups, rows, heads, slots, pieces, last, columns, chunk):
    local, gathered, halves = refs[:2], refs[2 : 2 + groups], refs[2 + groups : 4 + groups]
    weight_in, x_ref, free_total, same, other, *rest = refs[4 + groups :]
    own = rest.pop(0) if last else None
    mixed, high, total, sems = rest[len(pieces) :]
    copies = fetch(weight_in, pieces, rest, sems, columns)

    @region
    def _():
        flat, each = rows * heads, (slots + 1) * heads
        me = lax.axis_index("group")
        first, second = me * rows, jnp.bitwise_xor(me, 1) * rows
        free = jnp.zeros((heads, LANES), f32)
        found = []
        for part in gathered:
            for k in range(0, part.shape[0], each):
                stats = join_stats(part[k + slots * heads : k + each, :])
                free = free + stats
                for s in range(slots):
                    owner = stats[0, 2 * slots + s].astype(jnp.int32)
                    found.append((part, k, s, stats, owner))
        free_total[0] = free[0, 3 * slots].astype(jnp.int32)
        for i in range(2):
            high[i * flat : (i + 1) * flat, :] = local[i][flat : 2 * flat, :]
        slot_stats = []
        for part, k, s, stats, owner in found:
            in_first = (owner >= first) & (owner < first + rows)
            in_second = (owner >= second) & (owner < second + rows)
            row = jnp.where(
                in_first, owner - first, jnp.where(in_second, owner - second + rows, 0)
            )
            mine = in_first | in_second
            at = pl.ds(pl.multiple_of(row * heads, heads), heads)
            slot_high = jnp.broadcast_to(stats[:, s : s + 1], (heads, LANES))
            slot_total = jnp.broadcast_to(stats[:, slots + s : slots + s + 1], (heads, LANES))
            slot_stats.append((part, k + s * heads, mine, at, slot_high, slot_total))
            high[at, :] = jnp.maximum(high[at, :], jnp.where(mine, slot_high, far_below))
        for i in range(2):
            at = slice(i * flat, (i + 1) * flat)
            keep = jnp.exp2(local[i][flat : 2 * flat, :] - high[at, :])
            mixed[at, :] = keep * local[i][:flat, :]
            total[at, :] = keep * local[i][2 * flat :, :]
        for part, k, mine, at, slot_high, slot_total in slot_stats:
            add = jnp.where(mine, jnp.exp2(jnp.minimum(slot_high - high[at, :], 0.0)), 0.0)
            mixed[at, :] = mixed[at, :] + add * part[k : k + heads, :].astype(f32)
            total[at, :] = total[at, :] + add * slot_total
        mixed[...] = mixed[...] / total[...]
        for h in range(heads):
            x_ref[:, h * HEAD_DIM : (h + 1) * HEAD_DIM] = mixed[
                pl.ds(h, 2 * rows, stride=heads), :
            ].astype(bf16)

    @region
    def _():
        project(x_ref[...], halves, same, other, chunk, own)

    for copy in copies:
        copy.wait()


def project_kernel(x_ref, *refs, pieces, last, columns, chunk):
    halves = refs[:2]
    weight_in, same, other, *rest = refs[2:]
    own = rest.pop(0) if last else None
    copies = fetch(weight_in, pieces, rest, rest[-1], columns)
    region(lambda: project(x_ref[...], halves, same, other, chunk, own))
    for copy in copies:
        copy.wait()


def pick_kernel(even, odd, out):
    first = lax.axis_index("group") % 2 == 0

    @pl.when(first)
    def _():
        out[...] = even[...]

    @pl.when(jnp.logical_not(first))
    def _():
        out[...] = odd[...]


def sum_kernel(own, crossed, *refs):
    total = jnp.where(lax.axis_index("group") % 2 == 0, own[...], crossed[...].astype(f32))
    for part in refs[:-1]:
        total = total + part[...].astype(f32)
    refs[-1][...] = total.astype(bf16)


def send_block(value, step, crossed):
    groups, tp = lax.axis_size("group"), lax.axis_size("tp")
    pairs = [
        (g * tp + z, g * tp + (z ^ step_mask(g ^ crossed, step)))
        for g in range(groups)
        for z in range(tp)
    ]
    return lax.ppermute(value, ("group", "tp"), pairs)


def swap(value, axis, mask):
    size = lax.axis_size(axis)
    return lax.ppermute(value, axis, [(i, i ^ mask) for i in range(size)])


def gather_group(value):
    groups = lax.axis_size("group")
    found = [None] * groups
    found[0] = value
    found[1] = swap(value, "group", 1)
    for k in range(2, groups, 2):
        found[k] = swap(value, "group", k)
    for k in range(2, groups, 2):
        found[k + 1] = swap(found[k], "group", 1)
    return found


def step(
    queries,
    cache_keys,
    cache_values,
    pool_keys,
    pool_values,
    row_lengths,
    slot_owner,
    slot_fill,
    free_counts,
    out_weight,
):
    groups, tp = lax.axis_size("group"), lax.axis_size("tp")
    rows, width = queries.shape
    heads = width // HEAD_DIM
    kv_heads = cache_keys.shape[2] // HEAD_DIM
    slots, positions = pool_keys.shape[:2]
    columns = out_weight.shape[1] // tp
    chunk = math.gcd(columns, 2048)
    sizes = dict(rows=rows, heads=heads)

    shards = gather_group(queries)
    out_weight = pltpu.with_memory_space_constraint(out_weight, pltpu.MemorySpace.HBM)
    copies = pltpu.SemaphoreType.DMA

    order = list(range(tp // 2 - 1, -1, -1))
    pieces = [(step, half) for step in order for half in range(2)]
    held = jax.ShapeDtypeStruct((width // 2, columns), out_weight.dtype)
    piece_bytes = width * columns
    weights = {}

    def take(count):
        taken = pieces[:count]
        del pieces[:count]
        return taken

    token = call(open_kernel, jax.ShapeDtypeStruct((8, LANES), f32), [HBM], vmem=1 << 20)(
        out_weight
    )
    taken = take(1)
    local, *more = call(
        lambda *refs, taken=taken: local_kernel(
            *refs, kv_heads=kv_heads, pieces=taken, columns=columns, **sizes
        ),
        [
            jax.ShapeDtypeStruct((3 * rows * heads, LANES), f32),
        ]
        + [held] * len(taken),
        [SMEM, VMEM, VMEM, VMEM, HBM, VMEM],
        scratch=[
            pltpu.VMEM((rows * heads, HEAD_DIM), f32),
            pltpu.VMEM((rows, heads, cache_keys.shape[1]), f32),
            pltpu.VMEM((rows, heads, cache_keys.shape[1]), bf16),
            copies((1,)),
        ],
        moved=2 * (cache_keys.size + cache_values.size),
        vmem=4 << 20,
    )(row_lengths, queries, cache_keys, cache_values, out_weight, token)
    weights.update(zip(taken, more))
    pair_local = swap(local, "group", 1)

    taken = take(1)
    packed, *more = call(
        lambda *refs, taken=taken: slot_kernel(
            *refs,
            groups=groups,
            kv_heads=kv_heads,
            slots=slots,
            chunk=math.gcd(positions, 512),
            pieces=taken,
            columns=columns,
            **sizes,
        ),
        [jax.ShapeDtypeStruct(((slots + 1) * heads, LANES), bf16)] + [held] * len(taken),
        [SMEM] * 3 + [VMEM] * (groups + 2) + [HBM],
        scratch=[
            pltpu.VMEM((slots * heads, HEAD_DIM), f32),
            pltpu.VMEM((slots, heads, positions), f32),
            pltpu.VMEM((slots, heads, positions), bf16),
            copies((1,)),
        ],
        moved=2 * (pool_keys.size + pool_values.size),
        vmem=4 << 20,
    )(slot_owner, slot_fill, free_counts, *shards, pool_keys, pool_values, out_weight)
    weights.update(zip(taken, more))

    far = gather_group(packed)
    taken = take(1)
    more = call(
        lambda *refs, taken=taken: fetch_kernel(*refs, pieces=taken, columns=columns),
        [held] * len(taken),
        [HBM, pl.BlockSpec(memory_space=pl.ANY)],
        scratch=[copies((1,))],
        moved=piece_bytes,
        vmem=1 << 20,
    )(out_weight, packed)
    weights.update(zip(taken, more))

    block = jax.ShapeDtypeStruct((rows, columns), bf16)
    whole = jax.ShapeDtypeStruct((rows, columns), f32)
    received = []
    for i, step in enumerate(order):
        last = step == 0
        taken = take(max(0, len(pieces) - 2 * (len(order) - 2 - i)))
        outs = [block] * 2 + [whole] * last + [held] * len(taken)
        settings = dict(pieces=taken, last=last, columns=columns, chunk=chunk)
        halves = [weights[step, half] for half in range(2)]
        moved = piece_bytes * max(2, len(taken))
        if i == 0:
            x, free_total, same, other, *more = call(
                lambda *refs: combine_kernel(
                    *refs, groups=groups, slots=slots, **settings, **sizes
                ),
                [
                    jax.ShapeDtypeStruct((2 * rows, width), bf16),
                    jax.ShapeDtypeStruct((1,), jnp.int32),
                ]
                + outs,
                [VMEM] * (4 + groups) + [HBM],
                out_specs=[VMEM, SMEM] + [VMEM] * len(outs),
                scratch=[pltpu.VMEM((2 * rows * heads, LANES), f32)] * 3
                + [copies((max(1, len(taken)),))],
                moved=moved,
            )(local, pair_local, *far, *halves, out_weight)
        else:
            same, other, *more = call(
                lambda *refs, settings=settings: project_kernel(*refs, **settings),
                outs,
                [VMEM] * 3 + [HBM],
                scratch=[copies((max(1, len(taken)),))],
                moved=moved,
                vmem=4 << 20,
            )(x, *halves, out_weight)
        if last:
            own = more.pop(0)
        weights.update(zip(taken, more))
        crossed = swap(other, "group", 1)
        if last:
            leaving = call(pick_kernel, block, [VMEM] * 2, vmem=1 << 20)(crossed, same)
            received.append(swap(leaving, "tp", 1))
        else:
            received.append(send_block(same, step, 0))
            received.append(send_block(crossed, step, 1))
    mixed_out = call(sum_kernel, block, [VMEM] * (2 + len(received)))(own, crossed, *received)
    return (mixed_out, free_total)


def solution(mesh):
    in_specs = (
        P("group", "tp"),
        P("group", None, "tp"),
        P("group", None, "tp"),
        P("group", None, "tp"),
        P("group", None, "tp"),
        P("group"),
        P("group"),
        P("group"),
        P("group"),
        P("tp", None),
    )
    out_specs = (P("group", "tp"), P())
    return jax.shard_map(step, mesh=mesh, in_specs=in_specs, out_specs=out_specs, check_vma=False)
```
